32 devices in a mesh: dp: 2 (over x), row: 4 (over y, core), col: 4 (over z).
Axes of the slice: x: 2, y: 2, z: 4, core: 2. Of those that a mesh axis runs over, the one named last changes fastest.
Arguments:
- tokens_in: bfloat16 [16384, 1024], P(('dp', 'col'), 'row'), may hold values from -6 to 6
- cotangent: bfloat16 [16384, 1024], P(('dp', 'col'), 'row'), may hold values from -6 to 6
- doc_lengths: int32 [8, 6], P(('dp', 'row')), may hold values from 1 to 1024, 2048 in all within a row
- mixer_gain: bfloat16 [1024], P('row'), may hold values from 0.099609375 to 1.8984375
- w_query: bfloat16 [1024, 512], P('row', 'col'), may hold values from -0.1875 to 0.1875
- w_key: bfloat16 [1024, 512], P('row', 'col'), may hold values from -0.1875 to 0.1875
- w_value: bfloat16 [1024, 1024], P('row', 'col'), may hold values from -0.1875 to 0.1875
- w_outgate: bfloat16 [1024, 1024], P('row', 'col'), may hold values from -0.1875 to 0.1875
- w_rank_in: bfloat16 [1024, 16], P('row'), may hold values from -0.1875 to 0.1875
- w_rank_out: bfloat16 [16, 512], P(None, 'col'), may hold values from -1.5 to 1.5
- decay_bias: bfloat16 [512], P('col'), may hold values from -1 to 6
- head_gain: bfloat16 [256], replicated, may hold values from 0.099609375 to 1.8984375
- w_output: bfloat16 [1024, 1024], P('col', 'row'), may hold values from -0.1875 to 0.1875
- ffn_gain: bfloat16 [1024], P('row'), may hold values from 0.099609375 to 1.8984375
- w_gate: bfloat16 [1024, 2816], P('row', 'col'), may hold values from -0.1875 to 0.1875
- w_up: bfloat16 [1024, 2816], P('row', 'col'), may hold values from -0.1875 to 0.1875
- w_down: bfloat16 [2816, 1024], P('col', 'row'), may hold values from -0.109375 to 0.109375
Outputs:
- output_rows: bfloat16 [16384, 1024], P(('dp', 'col'), 'row')
- grad_tokens: float32 [16384, 1024], P(('dp', 'col'), 'row')
- grad_mixer_gain: float32 [1024], P('row')
- grad_w_query: float32 [1024, 512], P('row', 'col')
- grad_w_key: float32 [1024, 512], P('row', 'col')
- grad_w_value: float32 [1024, 1024], P('row', 'col')
- grad_w_outgate: float32 [1024, 1024], P('row', 'col')
- grad_w_rank_in: float32 [1024, 16], P('row')
- grad_w_rank_out: float32 [16, 512], P(None, 'col')
- grad_decay_bias: float32 [512], P('col')
- grad_head_gain: float32 [256], replicated
- grad_w_output: float32 [1024, 1024], P('col', 'row')
- grad_ffn_gain: float32 [1024], P('row')
- grad_w_gate: float32 [1024, 2816], P('row', 'col')
- grad_w_up: float32 [1024, 2816], P('row', 'col')
- grad_w_down: float32 [2816, 1024], P('col', 'row')
The draws below stay inside these ranges and needn't reach their ends.
Inputs may be any that keep to these rules, and one draw needn't show every extreme that they name: `doc_lengths`: each row sums to 2048.
All inputs are finite; a program needn't handle non-finite values.
Results may differ from the reference program's by a relative error of at most 0.015.
Values may be sent and summed in bfloat16 or wider, within the bound.
No kernel may reach another device: no remote copies, remote signals or barrier semaphores. Data moves between devices by JAX's collectives and lax.ppermute only.
A program may use at most 256 MiB of HBM per device.

```python
import math
from functools import partial
import jax
import jax.numpy as jnp
import numpy as np
from jax import lax

D = 1024
HEADS = 4
DK = 512
DV = 1024
RANK = 16
FF = 2816
SEQ_LEN = 2048
SPAN = 64
DOCS = 6
HK = 128
HV = 256
TOKENS = 16384
NSEQ = 8


def block_scale(key, shape, pieces, smallest, largest):
    def one(axis_at, shards_of):
        draws = jax.random.uniform(jax.random.fold_in(jax.random.fold_in(key, 6), axis_at), (shards_of,), jnp.float32, smallest / len(pieces), largest / len(pieces))
        return jnp.repeat(jnp.exp(draws), shape[axis_at] // shards_of).reshape((-1,) + (1,) * (len(shape) - axis_at - 1))

    loudness = one(*pieces[0])
    for cut in pieces[1:]:
        loudness = loudness * one(*cut)
    return loudness


def profile(number_of, total, limit, lean):
    weights = [(1 << 20) // math.isqrt(rank ** lean) + 1 for rank in range(2, number_of + 1)]
    rest, holding = total - limit - (number_of - 1), [1] * (number_of - 1)
    while rest > 0:
        candidates = [i for i in range(number_of - 1) if holding[i] < limit]
        mass, budget = sum([weights[i] for i in candidates]), rest
        for i in candidates:
            more = min(limit - holding[i], max(1, budget * weights[i] // mass), rest)
            holding[i] = holding[i] + more
            rest = rest - more
    return np.array([limit] + holding)


def uneven_parts(key, amount, total, most, lean):
    if amount == 2:
        one = jax.random.randint(key, (), max(1, total - most), min(most, total - 1) + 1)
        return jnp.stack([one, total - one])
    tallies = jnp.asarray(profile(amount, total, most, lean), jnp.int32)
    pairs = (amount - 1) // 2
    donor, sink = tallies[1:1 + 2 * pairs:2], tallies[2:2 + 2 * pairs:2]
    margin = jnp.minimum(donor - 1, most - sink)
    passed = jax.random.randint(jax.random.fold_in(key, 1), (pairs,), 0, 1 << 20) % (margin + 1)
    tallies = tallies.at[1:1 + 2 * pairs:2].set(donor - passed).at[2:2 + 2 * pairs:2].set(sink + passed)
    return tallies[jax.random.permutation(jax.random.fold_in(key, 2), amount)]


def gaussian(own_key, dims, deviation, reach, pieces=(), kind=jnp.bfloat16):
    level = block_scale(own_key, dims, pieces, -0.22, 0.18) if pieces else 1.0
    values = jax.random.normal(own_key, dims, jnp.float32) * deviation * level
    return jnp.minimum(jnp.maximum(values, -reach), reach).astype(kind)


def setup_inputs(seed: int = 0) -> dict:
    streams_of = jax.random.split(jax.random.key(seed), 18)
    return {
        "tokens_in": gaussian(streams_of[0], (TOKENS, D), 1.0, 6.0, ((0, 8), (1, 4))),
        "cotangent": gaussian(streams_of[1], (TOKENS, D), 1.0, 6.0, ((0, 8), (1, 4))),
        "doc_lengths": jax.vmap(lambda own: uneven_parts(own, DOCS, SEQ_LEN, SEQ_LEN // 2, 1))(jax.random.split(streams_of[2], NSEQ)).reshape((NSEQ, DOCS)).astype(jnp.int32),
        "mixer_gain": jnp.clip(1.0 + 0.18 * jax.random.normal(streams_of[3], (D,), jnp.float32), 0.099609375, 1.8984375).astype(jnp.bfloat16),
        "w_query": gaussian(streams_of[4], (D, DK), D ** -0.5, 0.1875, ((0, 4), (1, 4))),
        "w_key": gaussian(streams_of[5], (D, DK), D ** -0.5, 0.1875, ((0, 4), (1, 4))),
        "w_value": gaussian(streams_of[6], (D, DV), D ** -0.5, 0.1875, ((0, 4), (1, 4))),
        "w_outgate": gaussian(streams_of[7], (D, DV), D ** -0.5, 0.1875, ((0, 4), (1, 4))),
        "w_rank_in": gaussian(streams_of[8], (D, RANK), D ** -0.5, 0.1875, ((0, 4),)),
        "w_rank_out": gaussian(streams_of[9], (RANK, DK), RANK ** -0.5, 1.5, ((1, 4),)),
        "decay_bias": jnp.clip(-1.0 + 7.0 * jax.random.uniform(streams_of[10], (DK,), jnp.float32) ** block_scale(streams_of[10], (DK,), ((0, 4),), -0.2, 0.2), -1.0, 6.0).astype(jnp.bfloat16),
        "head_gain": jnp.clip(1.0 + 0.18 * jax.random.normal(streams_of[11], (HV,), jnp.float32), 0.099609375, 1.8984375).astype(jnp.bfloat16),
        "w_output": gaussian(streams_of[12], (DV, D), DV ** -0.5, 0.1875, ((0, 4), (1, 4))),
        "ffn_gain": jnp.clip(1.0 + 0.18 * jax.random.normal(streams_of[13], (D,), jnp.float32), 0.099609375, 1.8984375).astype(jnp.bfloat16),
        "w_gate": gaussian(streams_of[14], (D, FF), D ** -0.5, 0.1875, ((0, 4), (1, 4))),
        "w_up": gaussian(streams_of[15], (D, FF), D ** -0.5, 0.1875, ((0, 4), (1, 4))),
        "w_down": gaussian(streams_of[16], (FF, D), FF ** -0.5, 0.109375, ((0, 4), (1, 4))),
    }


@jax.custom_vjp
def low(v):
    return lax.optimization_barrier(v.astype(jnp.bfloat16)).astype(jnp.float32)

@jax.custom_vjp
def low_back(v):
    return v

def low_keep(v):
    return (low(v), None)

def low_pass(kept, grad):
    return (grad,)

def back_keep(v):
    return (v, None)

def back_low(kept, grad):
    return (low(grad),)
low.defvjp(low_keep, low_pass)
low_back.defvjp(back_keep, back_low)
exact_mode = lax.Precision.HIGHEST
norm_eps = 1e-05
head_eps = 1.0

def matmul(left, right):
    return jnp.dot(left, right, precision=exact_mode, preferred_element_type=jnp.float32)

def rms_scale(values, epsilon):
    return values * lax.rsqrt(lax.optimization_barrier(jnp.mean(values * values, axis=-1, keepdims=True)) + epsilon)

def segment_ids(doc_lengths, length):
    starts = jnp.cumsum(doc_lengths, axis=-1, dtype=jnp.int32) - doc_lengths
    places = jnp.arange(length, dtype=jnp.int32)
    inside = (starts[:, None, :] <= places[None, :, None]).astype(jnp.int32)
    return (lax.optimization_barrier(jnp.sum(inside, axis=-1)) - 1).astype(jnp.int32)

def span_attend(queries, key_rows, value_rows, log_decay, segments):
    batch, length, head_count, key_dim = queries.shape
    value_dim = value_rows.shape[-1]
    spans = length // SPAN
    queries = queries.reshape(batch, spans, SPAN, head_count, key_dim)
    key_rows = key_rows.reshape(batch, spans, SPAN, head_count, key_dim)
    value_rows = value_rows.reshape(batch, spans, SPAN, head_count, value_dim)
    log_decay = log_decay.reshape(batch, spans, SPAN, head_count, key_dim)
    segments = segments.reshape(batch, spans, SPAN)
    cumulative = jnp.cumsum(log_decay, axis=2)
    final_log = cumulative[:, :, -1:]
    q_scaled = queries * jnp.exp(cumulative)
    k_scaled = key_rows * jnp.exp(-cumulative)
    k_to_end = key_rows * jnp.exp(final_log - cumulative)
    places = jnp.arange(SPAN, dtype=jnp.int32)
    causal = places[:, None] >= places[None, :]
    allowed = ((segments[..., :, None] == segments[..., None, :]) & causal).astype(jnp.float32)
    scores = jnp.einsum('bnihk,bnjhk->bnhij', q_scaled, k_scaled, precision=exact_mode) * allowed[:, :, None]
    within = jnp.einsum('bnhij,bnjhv->bnihv', scores, value_rows, precision=exact_mode)
    seg_last = segments[:, :, -1]
    tail_mask = (segments == seg_last[..., None]).astype(jnp.float32)
    update = jnp.einsum('bnjhk,bnjhv->bnhkv', k_to_end * tail_mask[..., None, None], value_rows, precision=exact_mode)
    seg_prev = jnp.concatenate([jnp.full((batch, 1), -1, jnp.int32), seg_last[:, :-1].astype(jnp.int32)], axis=1)
    carry_on = (seg_last == seg_prev).astype(jnp.float32)
    fade_out = jnp.exp(final_log[:, :, 0])

    def advance(carried, inputs):
        fade_now, keep_now, update_now = inputs
        before = carried
        carried = carried * (fade_now * keep_now[:, None, None])[..., None] + update_now
        return (carried, before)
    start_state = jnp.zeros((batch, head_count, key_dim, value_dim), jnp.float32)
    _, states = lax.scan(advance, start_state, (jnp.moveaxis(fade_out, 1, 0), jnp.moveaxis(carry_on, 1, 0), jnp.moveaxis(update, 1, 0)))
    states = jnp.moveaxis(states, 0, 1)
    reads_old = (segments == seg_prev[..., None]).astype(jnp.float32)
    across = jnp.einsum('bnihk,bnhkv->bnihv', q_scaled * reads_old[..., None, None], states, precision=exact_mode)
    return (within + across).reshape(batch, length, head_count, value_dim)

def attend_block(packed):
    return span_attend(*packed)

def mixer_whole(queries, key_rows, value_rows, gate_rows, decay_pre, gain_head, segments):
    row_count = queries.shape[0]
    log_decay = jax.nn.log_sigmoid(decay_pre) / 16.0
    per_block = 2 if segments.shape[0] % 2 == 0 else 1
    blocks = segments.shape[0] // per_block

    def shaped(array_in, last_dim):
        return array_in.reshape(blocks, per_block, SEQ_LEN, HEADS, last_dim)
    attended = lax.map(jax.checkpoint(attend_block), (shaped(queries * HK ** (-0.5), HK), shaped(key_rows, HK), shaped(value_rows, HV), shaped(log_decay, HK), segments.reshape(blocks, per_block, SEQ_LEN)))
    attended = attended.reshape(row_count, HEADS, HV)
    normed = rms_scale(attended, head_eps) * gain_head
    return normed.reshape(row_count, DV) * jax.nn.silu(gate_rows)

def layer(inputs, mixer_gain, w_query, w_key, w_value, w_outgate, w_rank_in, w_rank_out, decay_bias, head_gain, w_output, ffn_gain, w_gate, w_up, w_down, segments):
    first = low(rms_scale(inputs, norm_eps) * mixer_gain)
    queries = low_back(matmul(first, w_query))
    key_rows = low_back(matmul(first, w_key))
    value_rows = low_back(matmul(first, w_value))
    gate_rows = low_back(matmul(first, w_outgate))
    rank_rows = matmul(first, w_rank_in)
    decay_pre = low_back(matmul(rank_rows, w_rank_out) + decay_bias)
    mixed = low(mixer_whole(queries, key_rows, value_rows, gate_rows, decay_pre, head_gain, segments))
    residual = inputs + low_back(matmul(mixed, w_output))
    second = low(rms_scale(residual, norm_eps) * ffn_gain)
    gate_pre = low_back(matmul(second, w_gate))
    up_pre = low_back(matmul(second, w_up))
    hidden = low(jax.nn.silu(gate_pre) * up_pre)
    return residual + low_back(matmul(hidden, w_down))

def reference(tokens_in, cotangent, doc_lengths, mixer_gain, w_query, w_key, w_value, w_outgate, w_rank_in, w_rank_out, decay_bias, head_gain, w_output, ffn_gain, w_gate, w_up, w_down):
    segments = segment_ids(doc_lengths, SEQ_LEN)
    params = tuple((arr_in.astype(jnp.float32) for arr_in in (tokens_in, mixer_gain, w_query, w_key, w_value, w_outgate, w_rank_in, w_rank_out, decay_bias, head_gain, w_output, ffn_gain, w_gate, w_up, w_down)))
    result, pullback = jax.vjp(partial(layer, segments=segments), *params)
    grads = pullback(cotangent.astype(jnp.float32))
    return (result.astype(jnp.bfloat16), grads[0], grads[1], grads[2], grads[3], grads[4], grads[5], grads[6], grads[7], grads[8], grads[9], grads[10], grads[11], grads[12], grads[13], grads[14])
```

```python
import jax
import jax.numpy as jnp
from jax import lax
from jax.experimental import pallas as pl
from jax.experimental.pallas import tpu as pltpu
from jax.sharding import PartitionSpec as P

D = 1024
SEQ_LEN = 2048
SPAN = 64
HK = 128
HV = 256
RANK = 16

exact_mode = lax.Precision.HIGHEST
norm_eps = 1e-05
head_eps = 1.0
f32 = jnp.float32
b16 = jnp.bfloat16
GRID = ("col", "row")
PACK = 2 * HK + HV + HK
NT = (((1,), (1,)), ((), ()))
TN = (((0,), (0,)), ((), ()))


def dot(left, right, dims=(((1,), (0,)), ((), ()))):
    return lax.dot_general(left, right, dims, preferred_element_type=f32)


def exchange(blocks):
    return lax.all_to_all(blocks, "row", 0, 0)


def span_parts(starts_ref, base, x):
    docs = starts_ref.shape[0]
    rows = lax.broadcasted_iota(jnp.int32, (SPAN, HK), 0) + base
    first = jnp.zeros((SPAN, HK), jnp.int32)
    last_first = jnp.int32(0)
    for d in range(docs):
        s = starts_ref[d]
        first = jnp.where(rows >= s, jnp.maximum(first, s), first)
        last_first = jnp.where(base + SPAN - 1 >= s, jnp.maximum(last_first, s), last_first)
    i = lax.broadcasted_iota(jnp.int32, (SPAN, SPAN), 0)
    j = lax.broadcasted_iota(jnp.int32, (SPAN, SPAN), 1)
    allowed = (j <= i) & (j + base >= first[:, :SPAN])
    reads = (first < base).astype(f32)
    tail = (rows >= last_first).astype(f32)
    keep = (last_first < base).astype(f32)
    q = x[:, :HK].astype(f32) * HK ** (-0.5)
    k = x[:, HK : 2 * HK].astype(f32)
    v = x[:, 2 * HK : 2 * HK + HV]
    lam = x[:, 2 * HK + HV :]
    tri = (j <= i).astype(b16)
    cum = dot(tri, lam)
    final = cum[SPAN - 1 :, :]
    e_pos = jnp.exp(cum)
    e_neg = jnp.exp(-cum)
    e_end = jnp.exp(final - cum)
    qs = (q * e_pos).astype(b16)
    ks = (k * e_neg).astype(b16)
    ke = (k * e_end * tail).astype(b16)
    qr = (qs.astype(f32) * reads).astype(b16)
    fade = jnp.exp(final) * keep
    scores = jnp.where(allowed, dot(qs, ks, NT), 0.0).astype(b16)
    return v, lam, e_pos, e_neg, e_end, qs, ks, ke, qr, fade, scores, allowed, reads, tail, i, j


def mix_forward(starts_ref, x_ref, o_ref, states_ref, carry_ref):
    step = pl.program_id(0)

    @pl.when(step == 0)
    def _():
        carry_ref[...] = jnp.zeros_like(carry_ref)

    rows = x_ref.shape[0]
    state = carry_ref[...]
    for n in range(rows // SPAN):
        at = pl.ds(n * SPAN, SPAN)
        part = span_parts(starts_ref, step * rows + n * SPAN, x_ref[at, :])
        v, ke, qr, fade, scores = part[0], part[7], part[8], part[9], part[10]
        low = state.astype(b16)
        states_ref[n] = low
        o_ref[at, :] = (dot(scores, v) + dot(qr, low, NT)).astype(b16)
        state = state * fade + dot(v, ke, TN)
    carry_ref[...] = state


def mix_backward(starts_ref, x_ref, do_ref, states_ref, out_ref, carry_ref):
    step = pl.program_id(0)
    steps = pl.num_programs(0)

    @pl.when(step == 0)
    def _():
        carry_ref[...] = jnp.zeros_like(carry_ref)

    rows = x_ref.shape[0]
    grad = carry_ref[...]
    for n in reversed(range(rows // SPAN)):
        at = pl.ds(n * SPAN, SPAN)
        (v, lam, e_pos, e_neg, e_end, qs, ks, ke, qr, fade, scores, allowed, reads, tail, i, j) = (
            span_parts(starts_ref, (steps - 1 - step) * rows + n * SPAN, x_ref[at, :])
        )
        do = do_ref[at, :]
        low = grad.astype(b16)
        before = states_ref[n]
        d_scores = jnp.where(allowed, dot(do, v, NT), 0.0).astype(b16)
        dv = dot(scores, do, TN) + dot(ke, low, NT)
        dqs = dot(d_scores, ks) + dot(do, before) * reads
        dks = dot(d_scores, qs, TN)
        dke = dot(v, low) * tail
        d_fade = jnp.sum(before.astype(f32) * grad, axis=0, keepdims=True)
        grad = grad * fade + dot(do, qr, TN)
        end_part = dke * ke.astype(f32)
        d_cum = dqs * qs.astype(f32) - dks * ks.astype(f32) - end_part
        d_final = jnp.sum(end_part, axis=0, keepdims=True) + d_fade * fade
        upper = (j >= i).astype(b16)
        high = d_cum.astype(b16)
        rest = (d_cum - high.astype(f32)).astype(b16)
        d_lam = dot(upper, high) + dot(upper, rest) + d_final
        d_zeta = d_lam * ((1.0 - jnp.exp(lam.astype(f32) * 16.0)) / 16.0)
        out_ref[at, :HK] = (dqs * e_pos * HK ** (-0.5)).astype(b16)
        out_ref[at, HK : 2 * HK] = (dks * e_neg + dke * e_end).astype(b16)
        out_ref[at, 2 * HK : 2 * HK + HV] = dv.astype(b16)
        out_ref[at, 2 * HK + HV :] = d_zeta.astype(b16)
    carry_ref[...] = grad


BLOCK = 512


def run_forward(starts, packed):
    rows = packed.shape[0]
    spans = BLOCK // SPAN
    return pl.pallas_call(
        mix_forward,
        out_shape=(
            jax.ShapeDtypeStruct((rows, HV), b16),
            jax.ShapeDtypeStruct((rows // SPAN, HV, HK), b16),
        ),
        grid=(rows // BLOCK,),
        in_specs=[
            pl.BlockSpec(memory_space=pltpu.SMEM),
            pl.BlockSpec((BLOCK, PACK), lambda s: (s, 0)),
        ],
        out_specs=(
            pl.BlockSpec((BLOCK, HV), lambda s: (s, 0)),
            pl.BlockSpec((spans, HV, HK), lambda s: (s, 0, 0)),
        ),
        scratch_shapes=[pltpu.VMEM((HV, HK), f32)],
        cost_estimate=pl.CostEstimate(
            flops=rows * 180000, bytes_accessed=rows * 2600, transcendentals=rows * 400
        ),
        name="mix_forward",
    )(starts, packed)


def run_backward(starts, packed, d_out, states):
    rows = packed.shape[0]
    spans = BLOCK // SPAN
    steps = rows // BLOCK
    return pl.pallas_call(
        mix_backward,
        out_shape=jax.ShapeDtypeStruct((rows, PACK), b16),
        grid=(steps,),
        in_specs=[
            pl.BlockSpec(memory_space=pltpu.SMEM),
            pl.BlockSpec((BLOCK, PACK), lambda s: (steps - 1 - s, 0)),
            pl.BlockSpec((BLOCK, HV), lambda s: (steps - 1 - s, 0)),
            pl.BlockSpec((spans, HV, HK), lambda s: (steps - 1 - s, 0, 0)),
        ],
        out_specs=pl.BlockSpec((BLOCK, PACK), lambda s: (steps - 1 - s, 0)),
        scratch_shapes=[pltpu.VMEM((HV, HK), f32)],
        cost_estimate=pl.CostEstimate(
            flops=rows * 500000, bytes_accessed=rows * 4200, transcendentals=rows * 600
        ),
        name="mix_backward",
    )(starts, packed, d_out, states)


def gather_blocks(block, rows, cols):
    whole = lax.all_gather(block, GRID, axis=0, tiled=True)
    return whole.reshape(cols, rows, block.shape[0], block.shape[1])


def scatter_blocks(blocks):
    flat = blocks.reshape(-1, blocks.shape[-1])
    return lax.psum_scatter(flat, GRID, scatter_dimension=0, tiled=True)


def batch_sum(part, pair):
    if pair == 2:
        other = lax.ppermute(part, "dp", [(0, 1), (1, 0)])
        return part.astype(f32) + other.astype(f32)
    return lax.psum(part, "dp").astype(f32)


def wide(blocks):
    c, r, a, b = blocks.shape
    return blocks.transpose(0, 2, 1, 3).reshape(c, a, r * b)


def split_wide(whole, r):
    c, a, b = whole.shape
    return whole.reshape(c, a, r, b // r).transpose(0, 2, 1, 3)


def make_body(dp, rows, cols):
    def per_device(
        tokens_in,
        cotangent,
        doc_lengths,
        mixer_gain,
        w_query,
        w_key,
        w_value,
        w_outgate,
        w_rank_in,
        w_rank_out,
        decay_bias,
        head_gain,
        w_output,
        ffn_gain,
        w_gate,
        w_up,
        w_down,
    ):
        feat = tokens_in.shape[1]
        count = tokens_in.shape[0] // rows
        narrow = 2 * HK + 2 * HV
        cross = [(a * cols + b, b * cols + a) for a in range(rows) for b in range(cols)]
        lengths = lax.ppermute(doc_lengths, ("row", "col"), cross)[0]
        starts = jnp.cumsum(lengths, dtype=jnp.int32) - lengths
        key_side = jnp.concatenate([w_rank_out.T, decay_bias[:, None]], axis=1)
        side = jnp.concatenate(
            [
                w_rank_in,
                mixer_gain[:, None],
                ffn_gain[:, None],
                jnp.pad(key_side, ((0, feat - HK), (0, 0))),
                jnp.zeros((feat, 128 - 2 * RANK - 3), b16),
            ],
            axis=1,
        )
        first_w = gather_blocks(
            jnp.concatenate([w_query, w_key, w_value, w_outgate, side], axis=1), rows, cols
        )
        out_w = gather_blocks(w_output, rows, cols)
        gate_w = gather_blocks(w_gate, rows, cols)
        up_w = gather_blocks(w_up, rows, cols)
        down_w = gather_blocks(w_down, rows, cols)
        extra = first_w[0, :, :, narrow:].reshape(D, 128)
        rank_in = extra[:, :RANK]
        gain_one = extra[:, RANK].astype(f32)
        gain_two = extra[:, RANK + 1].astype(f32)
        keys_extra = first_w[:, 0, :HK, narrow:]
        rank_out = keys_extra[:, :, RANK + 2 : 2 * RANK + 2].astype(f32)
        bias = keys_extra[:, :, 2 * RANK + 2].astype(f32)
        first_w = first_w.reshape(cols, D, narrow + 128)[:, :, :narrow]
        gate_w = gate_w.reshape(cols, D, -1)
        up_w = up_w.reshape(cols, D, -1)
        out_w = wide(out_w)
        down_w = wide(down_w)

        both = jnp.stack(
            [tokens_in.reshape(rows, count, feat), cotangent.reshape(rows, count, feat)], axis=1
        )
        both = exchange(both).transpose(1, 2, 0, 3).reshape(2, count, D)
        inputs = both[0].astype(f32)
        cot = both[1]
        inv_one = lax.rsqrt(jnp.mean(inputs * inputs, axis=1, keepdims=True) + norm_eps)
        normed_one = inputs * inv_one
        first = (normed_one * gain_one).astype(b16)
        proj = jnp.einsum("td,cdn->ctn", first, first_w, preferred_element_type=f32)
        rank_rows = dot(first, rank_in)
        zeta = (
            jnp.einsum("ts,cks->ctk", rank_rows, rank_out, precision=exact_mode)
            + bias[:, None, :]
        )
        lam = jax.nn.log_sigmoid(zeta) / 16.0
        gates = proj[:, :, 2 * HK + HV :]
        packed = jnp.concatenate([proj[:, :, : 2 * HK + HV], lam], axis=2).astype(b16)
        packed = exchange(packed).reshape(SEQ_LEN, PACK)
        attended, states = run_forward(starts, packed)
        heads = exchange(attended.reshape(rows, count, HV)).astype(f32)
        gain_head = head_gain.astype(f32)
        inv_head = lax.rsqrt(jnp.mean(heads * heads, axis=-1, keepdims=True) + head_eps)
        unit = heads * inv_head
        sig_out = jax.nn.sigmoid(gates)
        silu_out = gates * sig_out
        mixed = (unit * gain_head * silu_out).astype(b16)
        residual = inputs + jnp.einsum("ctv,cve->te", mixed, out_w, preferred_element_type=f32)
        inv_two = lax.rsqrt(jnp.mean(residual * residual, axis=1, keepdims=True) + norm_eps)
        normed_two = residual * inv_two
        second = (normed_two * gain_two).astype(b16)
        gate_pre = jnp.einsum("td,cdn->ctn", second, gate_w, preferred_element_type=f32)
        up_pre = jnp.einsum("td,cdn->ctn", second, up_w, preferred_element_type=f32)
        sig_gate = jax.nn.sigmoid(gate_pre)
        silu_gate = gate_pre * sig_gate
        hidden = (silu_gate * up_pre).astype(b16)

        grad_down = jnp.einsum("ctn,te->cne", hidden, cot, preferred_element_type=f32)
        grad_down = scatter_blocks(split_wide(grad_down.astype(b16), rows))
        d_hidden = jnp.einsum("te,cne->ctn", cot, down_w, preferred_element_type=f32)
        d_gate = (d_hidden * up_pre * sig_gate * (1.0 + gate_pre * (1.0 - sig_gate))).astype(b16)
        d_up = (d_hidden * silu_gate).astype(b16)
        grad_gate = jnp.einsum("td,ctn->cdn", second, d_gate, preferred_element_type=f32)
        grad_gate = scatter_blocks(grad_gate.astype(b16))
        grad_up = jnp.einsum("td,ctn->cdn", second, d_up, preferred_element_type=f32)
        grad_up = scatter_blocks(grad_up.astype(b16))
        out_rows = (
            residual + jnp.einsum("ctn,cne->te", hidden, down_w, preferred_element_type=f32)
        ).astype(b16)
        d_second = jnp.einsum(
            "ctn,cdn->td", d_gate, gate_w, preferred_element_type=f32
        ) + jnp.einsum("ctn,cdn->td", d_up, up_w, preferred_element_type=f32)
        part_two = jnp.sum(d_second * normed_two, axis=0)
        scaled_two = d_second * gain_two
        mean_two = jnp.mean(scaled_two * normed_two, axis=1, keepdims=True)
        d_resid = cot.astype(f32) + inv_two * (scaled_two - normed_two * mean_two)
        d_low = d_resid.astype(b16)
        grad_out = jnp.einsum("ctv,te->cve", mixed, d_low, preferred_element_type=f32)
        grad_out = scatter_blocks(split_wide(grad_out.astype(b16), rows))
        d_mixed = jnp.einsum("te,cve->ctv", d_low, out_w, preferred_element_type=f32)
        gated = d_mixed * silu_out
        part_head = jnp.sum(gated * unit, axis=(0, 1))
        d_gates = d_mixed * unit * gain_head * sig_out * (1.0 + gates * (1.0 - sig_out))
        d_unit = gated * gain_head
        d_heads = inv_head * (d_unit - unit * jnp.mean(d_unit * unit, axis=-1, keepdims=True))
        d_attended = exchange(d_heads.astype(b16)).reshape(SEQ_LEN, HV)
        d_packed = run_backward(starts, packed, d_attended, states)
        d_packed = exchange(d_packed.reshape(rows, count, PACK))
        d_zeta = d_packed[:, :, 2 * HK + HV :].astype(f32)
        d_proj = jnp.concatenate([d_packed[:, :, : 2 * HK + HV], d_gates.astype(b16)], axis=2)
        d_rank = jnp.einsum("ctk,cks->ts", d_zeta, rank_out, precision=exact_mode)
        d_first = jnp.einsum(
            "ctn,cdn->td", d_proj, first_w, preferred_element_type=f32
        ) + lax.dot_general(
            d_rank, rank_in.astype(f32), NT, precision=exact_mode, preferred_element_type=f32
        )
        part_one = jnp.sum(d_first * normed_one, axis=0)
        scaled_one = d_first * gain_one
        mean_one = jnp.mean(scaled_one * normed_one, axis=1, keepdims=True)
        grad_tokens = d_resid + inv_one * (scaled_one - normed_one * mean_one)
        grad_first = jnp.einsum("td,ctn->cdn", first, d_proj, preferred_element_type=f32)
        part_rank_in = lax.dot_general(
            first.astype(f32), d_rank, TN, precision=exact_mode, preferred_element_type=f32
        )
        part_rank_out = jnp.einsum("ctk,ts->cks", d_zeta, rank_rows, precision=exact_mode)
        part_bias = jnp.sum(d_zeta, axis=1)
        row_side = jnp.concatenate(
            [part_rank_in, part_one[:, None], part_two[:, None]], axis=1
        ).reshape(1, rows, feat, RANK + 2)
        col_side = jnp.concatenate([part_rank_out, part_bias[:, :, None]], axis=2)
        col_side = jnp.pad(col_side, ((0, 0), (0, feat - HK), (0, 0)))[:, None]
        gain_side = part_head.reshape(1, 1, feat, 1)
        whole = (cols, rows, feat)
        side_grad = jnp.concatenate(
            [
                jnp.broadcast_to(row_side, whole + (RANK + 2,)),
                jnp.broadcast_to(col_side, whole + (RANK + 1,)),
                jnp.broadcast_to(gain_side, whole + (1,)),
                jnp.zeros(whole + (128 - 2 * RANK - 4,), f32),
            ],
            axis=3,
        ).reshape(cols, D, 128)
        grad_first = jnp.concatenate([grad_first.astype(b16), side_grad.astype(b16)], axis=2)
        grad_first = scatter_blocks(grad_first)

        out_rows = exchange(out_rows.reshape(count, rows, feat).transpose(1, 0, 2))
        grad_tokens = exchange(
            grad_tokens.astype(b16).reshape(count, rows, feat).transpose(1, 0, 2)
        )
        grad_down = batch_sum(grad_down, dp)
        grad_gate = batch_sum(grad_gate, dp)
        grad_up = batch_sum(grad_up, dp)
        grad_out = batch_sum(grad_out, dp)
        grad_first = batch_sum(grad_first, dp)
        side_sum = grad_first[:, narrow:]
        return (
            out_rows.reshape(rows * count, feat),
            grad_tokens.reshape(rows * count, feat).astype(f32),
            side_sum[:, RANK],
            grad_first[:, :HK],
            grad_first[:, HK : 2 * HK],
            grad_first[:, 2 * HK : 2 * HK + HV],
            grad_first[:, 2 * HK + HV : narrow],
            side_sum[:, :RANK],
            side_sum[:HK, RANK + 2 : 2 * RANK + 2].T,
            side_sum[:HK, 2 * RANK + 2],
            side_sum[:, 2 * RANK + 3],
            grad_out,
            side_sum[:, RANK + 1],
            grad_gate,
            grad_up,
            grad_down,
        )

    return per_device


def solution(mesh):
    grid = P("row", "col")
    flipped = P("col", "row")
    tokens = P(("dp", "col"), "row")
    in_specs = (
        tokens,
        tokens,
        P(("dp", "row"), None),
        P("row"),
        grid,
        grid,
        grid,
        grid,
        P("row", None),
        P(None, "col"),
        P("col"),
        P(),
        flipped,
        P("row"),
        grid,
        grid,
        flipped,
    )
    out_specs = (
        tokens,
        tokens,
        P("row"),
        grid,
        grid,
        grid,
        grid,
        P("row", None),
        P(None, "col"),
        P("col"),
        P(),
        flipped,
        P("row"),
        grid,
        grid,
        flipped,
    )
    body = make_body(mesh.shape["dp"], mesh.shape["row"], mesh.shape["col"])
    return jax.shard_map(
        body, mesh=mesh, in_specs=in_specs, out_specs=out_specs, check_vma=False
    )
```

```python
import jax
import jax.numpy as jnp
from jax import lax
from jax.experimental import pallas as pl
from jax.experimental.pallas import tpu as pltpu
from jax.sharding import PartitionSpec as P

D = 1024
SEQ_LEN = 2048
SPAN = 64
HK = 128
HV = 256
RANK = 16

exact_mode = lax.Precision.HIGHEST
norm_eps = 1e-05
head_eps = 1.0
f32 = jnp.float32
b16 = jnp.bfloat16
GRID = ("col", "row")
PACK = 2 * HK + HV + HK
NT = (((1,), (1,)), ((), ()))
TN = (((0,), (0,)), ((), ()))


def dot(left, right, dims=(((1,), (0,)), ((), ()))):
    return lax.dot_general(left, right, dims, preferred_element_type=f32)


def exchange(blocks):
    return lax.all_to_all(blocks, "row", 0, 0)


def span_parts(starts_ref, base, x):
    docs = starts_ref.shape[0]
    rows = lax.broadcasted_iota(jnp.int32, (SPAN, HK), 0) + base
    first = jnp.zeros((SPAN, HK), jnp.int32)
    last_first = jnp.int32(0)
    for d in range(docs):
        s = starts_ref[d]
        first = jnp.where(rows >= s, jnp.maximum(first, s), first)
        last_first = jnp.where(base + SPAN - 1 >= s, jnp.maximum(last_first, s), last_first)
    i = lax.broadcasted_iota(jnp.int32, (SPAN, SPAN), 0)
    j = lax.broadcasted_iota(jnp.int32, (SPAN, SPAN), 1)
    allowed = (j <= i) & (j + base >= first[:, :SPAN])
    reads = (first < base).astype(f32)
    tail = (rows >= last_first).astype(f32)
    keep = (last_first < base).astype(f32)
    q = x[:, :HK].astype(f32) * HK ** (-0.5)
    k = x[:, HK : 2 * HK].astype(f32)
    v = x[:, 2 * HK : 2 * HK + HV]
    lam = x[:, 2 * HK + HV :]
    tri = (j <= i).astype(b16)
    cum = dot(tri, lam)
    final = cum[SPAN - 1 :, :]
    e_pos = jnp.exp(cum)
    e_neg = jnp.exp(-cum)
    e_end = jnp.exp(final - cum)
    qs = (q * e_pos).astype(b16)
    ks = (k * e_neg).astype(b16)
    ke = (k * e_end * tail).astype(b16)
    qr = (qs.astype(f32) * reads).astype(b16)
    fade = jnp.exp(final) * keep
    scores = jnp.where(allowed, dot(qs, ks, NT), 0.0).astype(b16)
    return v, lam, e_pos, e_neg, e_end, qs, ks, ke, qr, fade, scores, allowed, reads, tail, i, j


def mix_forward(starts_ref, x_ref, o_ref, states_ref, carry_ref):
    step = pl.program_id(0)

    @pl.when(step == 0)
    def _():
        carry_ref[...] = jnp.zeros_like(carry_ref)

    rows = x_ref.shape[0]
    state = carry_ref[...]
    for n in range(rows // SPAN):
        at = pl.ds(n * SPAN, SPAN)
        part = span_parts(starts_ref, step * rows + n * SPAN, x_ref[at, :])
        v, ke, qr, fade, scores = part[0], part[7], part[8], part[9], part[10]
        low = state.astype(b16)
        states_ref[n] = low
        o_ref[at, :] = (dot(scores, v) + dot(qr, low, NT)).astype(b16)
        state = state * fade + dot(v, ke, TN)
    carry_ref[...] = state


def mix_backward(starts_ref, x_ref, do_ref, states_ref, out_ref, carry_ref):
    step = pl.program_id(0)
    steps = pl.num_programs(0)

    @pl.when(step == 0)
    def _():
        carry_ref[...] = jnp.zeros_like(carry_ref)

    rows = x_ref.shape[0]
    grad = carry_ref[...]
    for n in reversed(range(rows // SPAN)):
        at = pl.ds(n * SPAN, SPAN)
        (v, lam, e_pos, e_neg, e_end, qs, ks, ke, qr, fade, scores, allowed, reads, tail, i, j) = (
            span_parts(starts_ref, (steps - 1 - step) * rows + n * SPAN, x_ref[at, :])
        )
        do = do_ref[at, :]
        low = grad.astype(b16)
        before = states_ref[n]
        d_scores = jnp.where(allowed, dot(do, v, NT), 0.0).astype(b16)
        dv = dot(scores, do, TN) + dot(ke, low, NT)
        dqs = dot(d_scores, ks) + dot(do, before) * reads
        dks = dot(d_scores, qs, TN)
        dke = dot(v, low) * tail
        d_fade = jnp.sum(before.astype(f32) * grad, axis=0, keepdims=True)
        grad = grad * fade + dot(do, qr, TN)
        end_part = dke * ke.astype(f32)
        d_cum = dqs * qs.astype(f32) - dks * ks.astype(f32) - end_part
        d_final = jnp.sum(end_part, axis=0, keepdims=True) + d_fade * fade
        upper = (j >= i).astype(b16)
        high = d_cum.astype(b16)
        rest = (d_cum - high.astype(f32)).astype(b16)
        d_lam = dot(upper, high) + dot(upper, rest) + d_final
        d_zeta = d_lam * ((1.0 - jnp.exp(lam.astype(f32) * 16.0)) / 16.0)
        out_ref[at, :HK] = (dqs * e_pos * HK ** (-0.5)).astype(b16)
        out_ref[at, HK : 2 * HK] = (dks * e_neg + dke * e_end).astype(b16)
        out_ref[at, 2 * HK : 2 * HK + HV] = dv.astype(b16)
        out_ref[at, 2 * HK + HV :] = d_zeta.astype(b16)
    carry_ref[...] = grad


BLOCK = 512


def run_forward(starts, packed):
    rows = packed.shape[0]
    spans = BLOCK // SPAN
    return pl.pallas_call(
        mix_forward,
        out_shape=(
            jax.ShapeDtypeStruct((rows, HV), b16),
            jax.ShapeDtypeStruct((rows // SPAN, HV, HK), b16),
        ),
        grid=(rows // BLOCK,),
        in_specs=[
            pl.BlockSpec(memory_space=pltpu.SMEM),
            pl.BlockSpec((BLOCK, PACK), lambda s: (s, 0)),
        ],
        out_specs=(
            pl.BlockSpec((BLOCK, HV), lambda s: (s, 0)),
            pl.BlockSpec((spans, HV, HK), lambda s: (s, 0, 0)),
        ),
        scratch_shapes=[pltpu.VMEM((HV, HK), f32)],
        cost_estimate=pl.CostEstimate(
            flops=rows * 180000, bytes_accessed=rows * 2600, transcendentals=rows * 400
        ),
        name="mix_forward",
    )(starts, packed)


def run_backward(starts, packed, d_out, states):
    rows = packed.shape[0]
    spans = BLOCK // SPAN
    steps = rows // BLOCK
    return pl.pallas_call(
        mix_backward,
        out_shape=jax.ShapeDtypeStruct((rows, PACK), b16),
        grid=(steps,),
        in_specs=[
            pl.BlockSpec(memory_space=pltpu.SMEM),
            pl.BlockSpec((BLOCK, PACK), lambda s: (steps - 1 - s, 0)),
            pl.BlockSpec((BLOCK, HV), lambda s: (steps - 1 - s, 0)),
            pl.BlockSpec((spans, HV, HK), lambda s: (steps - 1 - s, 0, 0)),
        ],
        out_specs=pl.BlockSpec((BLOCK, PACK), lambda s: (steps - 1 - s, 0)),
        scratch_shapes=[pltpu.VMEM((HV, HK), f32)],
        cost_estimate=pl.CostEstimate(
            flops=rows * 500000, bytes_accessed=rows * 4200, transcendentals=rows * 600
        ),
        name="mix_backward",
    )(starts, packed, d_out, states)


def gather_blocks(block, rows, cols):
    whole = lax.all_gather(block, GRID, axis=0, tiled=True)
    return whole.reshape(cols, rows, block.shape[0], block.shape[1])


def batch_sum(part, pair):
    if pair == 2:
        other = lax.ppermute(part, "dp", [(0, 1), (1, 0)])
        return part.astype(f32) + other.astype(f32)
    return lax.psum(part, "dp").astype(f32)


def swap(part, bit, rows):
    return lax.ppermute(part, "row", [(i, i ^ bit) for i in range(rows)])


def pair_features(whole, rows):
    feat = whole.shape[1] // rows
    me = lax.axis_index("row")

    def piece(bit):
        return lax.dynamic_slice_in_dim(whole, (me ^ bit) * feat, feat, 1)

    other = swap(jnp.stack([piece(1), piece(3)]), 1, rows)
    keep = jnp.concatenate([piece(0), other[0]], axis=0)
    send = jnp.concatenate([piece(2), other[1]], axis=0)
    return keep, send


def pair_tokens(blocks, rows):
    return jnp.concatenate([blocks, swap(blocks, 1, rows)], axis=1)


def weight_grad(features, blocks, rows, side=None):
    keep, send = features
    away = jnp.einsum("td,ctn->cdn", send, blocks, preferred_element_type=f32).astype(b16)
    if side is not None:
        away = jnp.concatenate([away, side[1]], axis=2)
    came = swap(away, 2, rows)
    held = jnp.einsum("td,ctn->cdn", keep, blocks, preferred_element_type=f32)
    if side is not None:
        held = jnp.concatenate([held, side[0]], axis=2)
    total = (held + came.astype(f32)).astype(b16)
    flat = total.reshape(-1, total.shape[-1])
    return lax.psum_scatter(flat, "col", scatter_dimension=0, tiled=True)


def make_body(dp, rows, cols):
    def per_device(
        tokens_in,
        cotangent,
        doc_lengths,
        mixer_gain,
        w_query,
        w_key,
        w_value,
        w_outgate,
        w_rank_in,
        w_rank_out,
        decay_bias,
        head_gain,
        w_output,
        ffn_gain,
        w_gate,
        w_up,
        w_down,
    ):
        feat = tokens_in.shape[1]
        count = tokens_in.shape[0] // rows
        narrow = 2 * HK + 2 * HV
        cross = [(a * cols + b, b * cols + a) for a in range(rows) for b in range(cols)]
        lengths = lax.ppermute(doc_lengths, ("row", "col"), cross)[0]
        starts = jnp.cumsum(lengths, dtype=jnp.int32) - lengths
        key_side = jnp.concatenate([w_rank_out.T, decay_bias[:, None]], axis=1)
        side = jnp.concatenate(
            [
                w_rank_in,
                mixer_gain[:, None],
                ffn_gain[:, None],
                jnp.pad(key_side, ((0, feat - HK), (0, 0))),
                jnp.zeros((feat, 128 - 2 * RANK - 3), b16),
            ],
            axis=1,
        )
        first_w = gather_blocks(
            jnp.concatenate([w_query, w_key, w_value, w_outgate, side], axis=1), rows, cols
        )
        late_w = gather_blocks(
            jnp.concatenate([w_gate, w_up, w_output.T, w_down.T], axis=1), rows, cols
        )
        extra = first_w[0, :, :, narrow:].reshape(D, 128)
        rank_in = extra[:, :RANK]
        gain_one = extra[:, RANK].astype(f32)
        gain_two = extra[:, RANK + 1].astype(f32)
        keys_extra = first_w[:, 0, :HK, narrow:]
        rank_out = keys_extra[:, :, RANK + 2 : 2 * RANK + 2].astype(f32)
        bias = keys_extra[:, :, 2 * RANK + 2].astype(f32)
        first_w = first_w.reshape(cols, D, narrow + 128)[:, :, :narrow]
        late_w = late_w.reshape(cols, D, -1)
        hid = w_gate.shape[1]
        late_w_hid = late_w[:, :, : 2 * hid]
        out_w = late_w[:, :, 2 * hid : 2 * hid + HV]
        down_w = late_w[:, :, 2 * hid + HV :]

        both = jnp.stack(
            [tokens_in.reshape(rows, count, feat), cotangent.reshape(rows, count, feat)], axis=1
        )
        both = exchange(both).transpose(1, 2, 0, 3).reshape(2, count, D)
        inputs = both[0].astype(f32)
        cot = both[1]
        inv_one = lax.rsqrt(jnp.mean(inputs * inputs, axis=1, keepdims=True) + norm_eps)
        normed_one = inputs * inv_one
        first = (normed_one * gain_one).astype(b16)
        proj = jnp.einsum("td,cdn->ctn", first, first_w, preferred_element_type=f32)
        rank_rows = dot(first, rank_in)
        zeta = (
            jnp.einsum("ts,cks->ctk", rank_rows, rank_out, precision=exact_mode)
            + bias[:, None, :]
        )
        lam = jax.nn.log_sigmoid(zeta) / 16.0
        gates = proj[:, :, 2 * HK + HV :]
        packed = jnp.concatenate([proj[:, :, : 2 * HK + HV], lam], axis=2).astype(b16)
        packed = exchange(packed).reshape(SEQ_LEN, PACK)
        attended, states = run_forward(starts, packed)
        heads = exchange(attended.reshape(rows, count, HV)).astype(f32)
        gain_head = head_gain.astype(f32)
        inv_head = lax.rsqrt(jnp.mean(heads * heads, axis=-1, keepdims=True) + head_eps)
        unit = heads * inv_head
        sig_out = jax.nn.sigmoid(gates)
        silu_out = gates * sig_out
        mixed = (unit * gain_head * silu_out).astype(b16)
        residual = inputs + jnp.einsum("ctv,cdv->td", mixed, out_w, preferred_element_type=f32)
        inv_two = lax.rsqrt(jnp.mean(residual * residual, axis=1, keepdims=True) + norm_eps)
        normed_two = residual * inv_two
        second = (normed_two * gain_two).astype(b16)
        pre = jnp.einsum("td,cdn->ctn", second, late_w_hid, preferred_element_type=f32)
        gate_pre = pre[:, :, :hid]
        up_pre = pre[:, :, hid:]
        sig_gate = jax.nn.sigmoid(gate_pre)
        silu_gate = gate_pre * sig_gate
        hidden = (silu_gate * up_pre).astype(b16)

        cot_pair = pair_features(cot, rows)
        grad_down = weight_grad(cot_pair, pair_tokens(hidden, rows), rows)
        d_hidden = jnp.einsum("td,cdn->ctn", cot, down_w, preferred_element_type=f32)
        d_gate = d_hidden * up_pre * sig_gate * (1.0 + gate_pre * (1.0 - sig_gate))
        d_up = d_hidden * silu_gate
        d_pre = jnp.concatenate([d_gate.astype(b16), d_up.astype(b16)], axis=2)
        grad_hid = weight_grad(pair_features(second, rows), pair_tokens(d_pre, rows), rows)
        out_rows = (
            residual + jnp.einsum("ctn,cdn->td", hidden, down_w, preferred_element_type=f32)
        ).astype(b16)
        d_second = jnp.einsum("ctn,cdn->td", d_pre, late_w_hid, preferred_element_type=f32)
        part_two = jnp.sum(d_second * normed_two, axis=0)
        scaled_two = d_second * gain_two
        mean_two = jnp.mean(scaled_two * normed_two, axis=1, keepdims=True)
        d_resid = cot.astype(f32) + inv_two * (scaled_two - normed_two * mean_two)
        d_low = d_resid.astype(b16)
        grad_out = weight_grad(pair_features(d_low, rows), pair_tokens(mixed, rows), rows)
        d_mixed = jnp.einsum("td,cdv->ctv", d_low, out_w, preferred_element_type=f32)
        gated = d_mixed * silu_out
        part_head = jnp.sum(gated * unit, axis=(0, 1))
        d_gates = d_mixed * unit * gain_head * sig_out * (1.0 + gates * (1.0 - sig_out))
        d_unit = gated * gain_head
        d_heads = inv_head * (d_unit - unit * jnp.mean(d_unit * unit, axis=-1, keepdims=True))
        d_attended = exchange(d_heads.astype(b16)).reshape(SEQ_LEN, HV)
        d_packed = run_backward(starts, packed, d_attended, states)
        d_packed = exchange(d_packed.reshape(rows, count, PACK))
        d_zeta = d_packed[:, :, 2 * HK + HV :].astype(f32)
        d_proj = jnp.concatenate([d_packed[:, :, : 2 * HK + HV], d_gates.astype(b16)], axis=2)
        d_rank = jnp.einsum("ctk,cks->ts", d_zeta, rank_out, precision=exact_mode)
        d_first = jnp.einsum(
            "ctn,cdn->td", d_proj, first_w, preferred_element_type=f32
        ) + lax.dot_general(
            d_rank, rank_in.astype(f32), NT, precision=exact_mode, preferred_element_type=f32
        )
        part_one = jnp.sum(d_first * normed_one, axis=0)
        scaled_one = d_first * gain_one
        mean_one = jnp.mean(scaled_one * normed_one, axis=1, keepdims=True)
        grad_tokens = d_resid + inv_one * (scaled_one - normed_one * mean_one)
        part_rank_in = lax.dot_general(
            first.astype(f32), d_rank, TN, precision=exact_mode, preferred_element_type=f32
        )
        part_rank_out = jnp.einsum("ctk,ts->cks", d_zeta, rank_rows, precision=exact_mode)
        part_bias = jnp.sum(d_zeta, axis=1)
        row_side = jnp.concatenate(
            [part_rank_in, part_one[:, None], part_two[:, None]], axis=1
        ).reshape(1, rows, feat, RANK + 2)
        col_side = jnp.concatenate([part_rank_out, part_bias[:, :, None]], axis=2)
        col_side = jnp.pad(col_side, ((0, 0), (0, feat - HK), (0, 0)))[:, None]
        gain_side = part_head.reshape(1, 1, feat, 1)
        whole = (cols, rows, feat)
        side_grad = jnp.concatenate(
            [
                jnp.broadcast_to(row_side, whole + (RANK + 2,)),
                jnp.broadcast_to(col_side, whole + (RANK + 1,)),
                jnp.broadcast_to(gain_side, whole + (1,)),
                jnp.zeros(whole + (128 - 2 * RANK - 4,), f32),
            ],
            axis=3,
        ).astype(b16)
        me = lax.axis_index("row")

        def side_piece(bit):
            return lax.dynamic_index_in_dim(side_grad, me ^ bit, 1, False)

        side_other = swap(jnp.stack([side_piece(1), side_piece(3)]), 1, rows).astype(f32)
        side_keep = side_piece(0).astype(f32) + side_other[0]
        side_send = (side_piece(2).astype(f32) + side_other[1]).astype(b16)
        grad_first = weight_grad(
            pair_features(first, rows), pair_tokens(d_proj, rows), rows, (side_keep, side_send)
        )

        out_rows = exchange(out_rows.reshape(count, rows, feat).transpose(1, 0, 2))
        grad_tokens = exchange(
            grad_tokens.astype(b16).reshape(count, rows, feat).transpose(1, 0, 2)
        )
        grad_down = batch_sum(grad_down, dp)
        grad_hid = batch_sum(grad_hid, dp)
        grad_out = batch_sum(grad_out, dp)
        grad_first = batch_sum(grad_first, dp)
        side_sum = grad_first[:, narrow:]
        return (
            out_rows.reshape(rows * count, feat),
            grad_tokens.reshape(rows * count, feat).astype(f32),
            side_sum[:, RANK],
            grad_first[:, :HK],
            grad_first[:, HK : 2 * HK],
            grad_first[:, 2 * HK : 2 * HK + HV],
            grad_first[:, 2 * HK + HV : narrow],
            side_sum[:, :RANK],
            side_sum[:HK, RANK + 2 : 2 * RANK + 2].T,
            side_sum[:HK, 2 * RANK + 2],
            side_sum[:, 2 * RANK + 3],
            grad_out.T,
            side_sum[:, RANK + 1],
            grad_hid[:, :hid],
            grad_hid[:, hid:],
            grad_down.T,
        )

    return per_device


def solution(mesh):
    grid = P("row", "col")
    flipped = P("col", "row")
    tokens = P(("dp", "col"), "row")
    in_specs = (
        tokens,
        tokens,
        P(("dp", "row"), None),
        P("row"),
        grid,
        grid,
        grid,
        grid,
        P("row", None),
        P(None, "col"),
        P("col"),
        P(),
        flipped,
        P("row"),
        grid,
        grid,
        flipped,
    )
    out_specs = (
        tokens,
        tokens,
        P("row"),
        grid,
        grid,
        grid,
        grid,
        P("row", None),
        P(None, "col"),
        P("col"),
        P(),
        flipped,
        P("row"),
        grid,
        grid,
        flipped,
    )
    body = make_body(mesh.shape["dp"], mesh.shape["row"], mesh.shape["col"])
    return jax.shard_map(
        body, mesh=mesh, in_specs=in_specs, out_specs=out_specs, check_vma=False
    )
```

```python
import jax
import jax.numpy as jnp
from jax import lax
from jax.experimental import pallas as pl
from jax.experimental.pallas import tpu as pltpu
from jax.sharding import PartitionSpec as P


D = 1024
SPAN = 64
HK = 128
HV = 256
RANK = 16

exact_mode = lax.Precision.HIGHEST
norm_eps = 1e-05
head_eps = 1.0
f32 = jnp.float32
b16 = jnp.bfloat16
GRID = ("col", "row")
NT = (((1,), (1,)), ((), ()))
TN = (((0,), (0,)), ((), ()))


def dot(left, right, dims=(((1,), (0,)), ((), ()))):
    return lax.dot_general(left, right, dims, preferred_element_type=f32)


def exchange(blocks):
    return lax.all_to_all(blocks, "row", 0, 0)


def span_parts(starts_ref, base, x):
    docs = starts_ref.shape[0] - 2
    rows = lax.broadcasted_iota(jnp.int32, (SPAN, HK), 0) + base
    first = jnp.zeros((SPAN, HK), jnp.int32)
    last_first = jnp.int32(0)
    for d in range(docs):
        s = starts_ref[d]
        first = jnp.where(rows >= s, jnp.maximum(first, s), first)
        last_first = jnp.where(base + SPAN - 1 >= s, jnp.maximum(last_first, s), last_first)
    i = lax.broadcasted_iota(jnp.int32, (SPAN, SPAN), 0)
    j = lax.broadcasted_iota(jnp.int32, (SPAN, SPAN), 1)
    allowed = (j <= i) & (j + base >= first[:, :SPAN])
    reads = (first < base).astype(f32)
    tail = (rows >= last_first).astype(f32)
    keep = (last_first < base).astype(f32)
    q = x[:, :HK].astype(f32) * HK ** (-0.5)
    k = x[:, HK : 2 * HK].astype(f32)
    v = x[:, 2 * HK : 2 * HK + HV]
    lam = x[:, 2 * HK + HV :]
    tri = (j <= i).astype(b16)
    cum = dot(tri, lam)
    final = cum[SPAN - 1 :, :]
    e_pos = jnp.exp(cum)
    e_neg = jnp.exp(-cum)
    e_end = jnp.exp(final - cum)
    qs = (q * e_pos).astype(b16)
    ks = (k * e_neg).astype(b16)
    ke = (k * e_end * tail).astype(b16)
    qr = (qs.astype(f32) * reads).astype(b16)
    fade = jnp.exp(final) * keep
    scores = jnp.where(allowed, dot(qs, ks, NT), 0.0).astype(b16)
    return v, lam, e_pos, e_neg, e_end, qs, ks, ke, qr, fade, scores, allowed, reads, tail, i, j


def span_base(info_ref, block, n):
    docs = info_ref.shape[0] - 2
    return info_ref[docs] * (2 * BLOCK) + block * BLOCK + n * SPAN


def mix_state(info_ref, x_ref, end_ref, carry_ref):
    block = pl.program_id(1)

    @pl.when(block == 0)
    def _():
        carry_ref[...] = jnp.zeros_like(carry_ref)

    state = carry_ref[...]
    for n in range(BLOCK // SPAN):
        part = span_parts(info_ref, span_base(info_ref, block, n), x_ref[pl.ds(n * SPAN, SPAN), :])
        state = state * part[9] + dot(part[0], part[7], TN)
    carry_ref[...] = state
    end_ref[...] = state


def mix_forward(info_ref, x_ref, start_ref, o_ref, states_ref, carry_ref):
    block = pl.program_id(1)

    @pl.when(block == 0)
    def _():
        carry_ref[...] = start_ref[...]

    state = carry_ref[...]
    for n in range(BLOCK // SPAN):
        at = pl.ds(n * SPAN, SPAN)
        part = span_parts(info_ref, span_base(info_ref, block, n), x_ref[at, :])
        v, ke, qr, fade, scores = part[0], part[7], part[8], part[9], part[10]
        low = state.astype(b16)
        states_ref[n] = low
        o_ref[at, :] = (dot(scores, v) + dot(qr, low, NT)).astype(b16)
        state = state * fade + dot(v, ke, TN)
    carry_ref[...] = state


def mix_grad_state(info_ref, x_ref, do_ref, end_ref, carry_ref):
    step = pl.program_id(1)

    @pl.when(step == 0)
    def _():
        carry_ref[...] = jnp.zeros_like(carry_ref)

    grad = carry_ref[...]
    for n in reversed(range(BLOCK // SPAN)):
        at = pl.ds(n * SPAN, SPAN)
        part = span_parts(info_ref, span_base(info_ref, 1 - step, n), x_ref[at, :])
        grad = grad * part[9] + dot(do_ref[at, :], part[8], TN)
    carry_ref[...] = grad
    end_ref[...] = grad


def mix_backward(info_ref, x_ref, do_ref, states_ref, start_ref, out_ref, carry_ref):
    step = pl.program_id(1)

    @pl.when(step == 0)
    def _():
        carry_ref[...] = start_ref[...]

    grad = carry_ref[...]
    for n in reversed(range(BLOCK // SPAN)):
        at = pl.ds(n * SPAN, SPAN)
        (v, lam, e_pos, e_neg, e_end, qs, ks, ke, qr, fade, scores, allowed, reads, tail, i, j) = (
            span_parts(info_ref, span_base(info_ref, 1 - step, n), x_ref[at, :])
        )
        do = do_ref[at, :]
        low = grad.astype(b16)
        before = states_ref[n]
        d_scores = jnp.where(allowed, dot(do, v, NT), 0.0).astype(b16)
        dv = dot(scores, do, TN) + dot(ke, low, NT)
        dqs = dot(d_scores, ks) + dot(do, before) * reads
        dks = dot(d_scores, qs, TN)
        dke = dot(v, low) * tail
        d_fade = jnp.sum(before.astype(f32) * grad, axis=0, keepdims=True)
        grad = grad * fade + dot(do, qr, TN)
        end_part = dke * ke.astype(f32)
        d_cum = dqs * qs.astype(f32) - dks * ks.astype(f32) - end_part
        d_final = jnp.sum(end_part, axis=0, keepdims=True) + d_fade * fade
        upper = (j >= i).astype(b16)
        high = d_cum.astype(b16)
        rest = (d_cum - high.astype(f32)).astype(b16)
        d_lam = dot(upper, high) + dot(upper, rest) + d_final
        d_zeta = d_lam * ((1.0 - jnp.exp(lam.astype(f32) * 16.0)) / 16.0)
        out_ref[at, :HK] = (dqs * e_pos * HK ** (-0.5)).astype(b16)
        out_ref[at, HK : 2 * HK] = (dks * e_neg + dke * e_end).astype(b16)
        out_ref[at, 2 * HK : 2 * HK + HV] = dv.astype(b16)
        out_ref[at, 2 * HK + HV :] = d_zeta.astype(b16)
    carry_ref[...] = grad


BLOCK = 512


def run_mix(kernel, reverse, work, info, operands, results):
    heads = operands[0].shape[1]

    def order(step):
        return 1 - step if reverse else step

    def spec(array):
        if len(array.shape) == 4:
            return pl.BlockSpec(
                (None, None) + array.shape[2:],
                lambda h, s, info_ref: (order(s) ^ info_ref[info_ref.shape[0] - 1], h, 0, 0),
            )
        if len(array.shape) == 5:
            return pl.BlockSpec(
                (None, None) + array.shape[2:], lambda h, s, info_ref: (order(s), h, 0, 0, 0)
            )
        return pl.BlockSpec((None,) + array.shape[1:], lambda h, s, info_ref: (h, 0, 0))

    return pl.pallas_call(
        kernel,
        out_shape=results,
        grid_spec=pltpu.PrefetchScalarGridSpec(
            num_scalar_prefetch=1,
            grid=(heads, 2),
            in_specs=[spec(array) for array in operands],
            out_specs=tuple(spec(array) for array in results),
            scratch_shapes=[pltpu.VMEM((HV, HK), f32)],
        ),
        cost_estimate=pl.CostEstimate(
            flops=work * 200000000, bytes_accessed=work * 4000000, transcendentals=work * 800000
        ),
    )(info, *operands)


def run_forward(info, packed, rows):
    pairs, heads, count = packed.shape[:3]
    state = jax.ShapeDtypeStruct((heads, HV, HK), f32)
    (end,) = run_mix(mix_state, False, 1, info, (packed,), (state,))
    begin = lax.ppermute(end, "row", [(0, 2), (1, 3)]) if rows else jnp.zeros_like(end)
    out = jax.ShapeDtypeStruct((pairs, heads, count, HV), b16)
    kept = jax.ShapeDtypeStruct((pairs, heads, count // SPAN, HV, HK), b16)
    return run_mix(mix_forward, False, 2, info, (packed, begin), (out, kept))


def run_backward(info, packed, d_out, states, rows):
    _, heads, _ = packed.shape[:3]
    state = jax.ShapeDtypeStruct((heads, HV, HK), f32)
    (end,) = run_mix(mix_grad_state, True, 1, info, (packed, d_out), (state,))
    begin = lax.ppermute(end, "row", [(2, 0), (3, 1)]) if rows else jnp.zeros_like(end)
    out = jax.ShapeDtypeStruct(packed.shape, b16)
    return run_mix(mix_backward, True, 4, info, (packed, d_out, states, begin), (out,))[0]


def gather_blocks(block, rows, cols):
    whole = lax.all_gather(block, GRID, axis=0, tiled=True)
    return whole.reshape(cols, rows, block.shape[0], block.shape[1])


def batch_sum(part, pair):
    if pair == 2:
        other = lax.ppermute(part, "dp", [(0, 1), (1, 0)])
        return part.astype(f32) + other.astype(f32)
    return lax.psum(part, "dp").astype(f32)


def swap(part, bit, rows):
    return lax.ppermute(part, "row", [(i, i ^ bit) for i in range(rows)])


def pair_features(whole, rows):
    feat = whole.shape[1] // rows
    me = lax.axis_index("row")

    def piece(bit):
        return lax.dynamic_slice_in_dim(whole, (me ^ bit) * feat, feat, 1)

    other = swap(jnp.stack([piece(1), piece(3)]), 1, rows)
    keep = jnp.concatenate([piece(0), other[0]], axis=0)
    send = jnp.concatenate([piece(2), other[1]], axis=0)
    return keep, send


def pair_tokens(blocks, rows):
    return jnp.concatenate([blocks, swap(blocks, 1, rows)], axis=1)


def to_heads(blocks, rows):
    parts = blocks.reshape((2, -1) + blocks.shape[1:])
    core = lax.axis_index("row") % 2
    mine = lax.dynamic_index_in_dim(parts, core, 0, False)
    away = lax.dynamic_index_in_dim(parts, 1 - core, 0, False)
    return jnp.stack([mine, swap(away, 1, rows)])


def to_tokens(parts, rows):
    other = swap(parts[1], 1, rows)
    core = lax.axis_index("row") % 2
    both = jnp.where(
        core == 0, jnp.stack([parts[0], other]), jnp.stack([other, parts[0]])
    )
    return both.reshape((-1,) + both.shape[2:])


def grad_part(features, blocks):
    return jnp.einsum("td,ctn->cdn", features, blocks, preferred_element_type=f32)


def col_sum(total):
    flat = total.reshape(-1, total.shape[-1])
    return lax.psum_scatter(flat, "col", scatter_dimension=0, tiled=True)


def after(value, *firsts):
    return lax.optimization_barrier((value,) + firsts)[0]


def make_body(dp, rows, cols):
    def per_device(
        tokens_in,
        cotangent,
        doc_lengths,
        mixer_gain,
        w_query,
        w_key,
        w_value,
        w_outgate,
        w_rank_in,
        w_rank_out,
        decay_bias,
        head_gain,
        w_output,
        ffn_gain,
        w_gate,
        w_up,
        w_down,
    ):
        feat = tokens_in.shape[1]
        count = tokens_in.shape[0] // rows
        narrow = 2 * HK + HV
        cross = [(a * cols + b, b * cols + a) for a in range(rows) for b in range(cols)]
        lengths = lax.ppermute(doc_lengths, ("row", "col"), cross)[0]
        starts = jnp.cumsum(lengths, dtype=jnp.int32) - lengths
        me = lax.axis_index("row")
        info = jnp.concatenate([starts, jnp.stack([me // 2, me % 2]).astype(jnp.int32)])
        key_side = jnp.concatenate([w_rank_out.T, decay_bias[:, None]], axis=1)
        side = jnp.concatenate(
            [
                w_rank_in,
                mixer_gain[:, None],
                ffn_gain[:, None],
                jnp.pad(key_side, ((0, feat - HK), (0, 0))),
                jnp.zeros((feat, 128 - 2 * RANK - 3), b16),
            ],
            axis=1,
        )
        first_w = gather_blocks(
            jnp.concatenate([w_query, w_key, w_value, side], axis=1), rows, cols
        )
        late_w = gather_blocks(
            jnp.concatenate(
                [
                    w_gate,
                    w_up,
                    w_output.T,
                    w_outgate,
                    w_down.T,
                    jnp.zeros((feat, -(3 * w_gate.shape[1]) % 128), b16),
                ],
                axis=1,
            ),
            rows,
            cols,
        )
        extra = first_w[0, :, :, narrow:].reshape(D, 128)
        rank_in = extra[:, :RANK]
        gain_one = extra[:, RANK].astype(f32)
        gain_two = extra[:, RANK + 1].astype(f32)
        keys_extra = first_w[:, 0, :HK, narrow:]
        rank_out = keys_extra[:, :, RANK + 2 : 2 * RANK + 2].astype(f32)
        bias = keys_extra[:, :, 2 * RANK + 2].astype(f32)
        first_w = first_w.reshape(cols, D, narrow + 128)[:, :, :narrow]
        late_w = late_w.reshape(cols, D, -1)
        hid = w_gate.shape[1]
        late_w_hid = late_w[:, :, : 2 * hid]
        out_w = late_w[:, :, 2 * hid : 2 * hid + HV]
        outgate_w = late_w[:, :, 2 * hid + HV : 2 * hid + 2 * HV]
        down_w = late_w[:, :, 2 * hid + 2 * HV : 3 * hid + 2 * HV]

        def features_whole(block):
            split = exchange(block.reshape(rows, count, feat))
            return split.transpose(1, 0, 2).reshape(count, D)

        inputs = features_whole(tokens_in).astype(f32)
        inv_one = lax.rsqrt(jnp.mean(inputs * inputs, axis=1, keepdims=True) + norm_eps)
        normed_one = inputs * inv_one
        first = (normed_one * gain_one).astype(b16)
        proj = jnp.einsum("td,cdn->ctn", first, first_w, preferred_element_type=f32)
        rank_rows = dot(first, rank_in)
        zeta = (
            jnp.einsum("ts,cks->ctk", rank_rows, rank_out, precision=exact_mode)
            + bias[:, None, :]
        )
        lam = jax.nn.log_sigmoid(zeta) / 16.0
        packed = jnp.concatenate([proj, lam], axis=2).astype(b16)
        packed = to_heads(packed, rows)
        attended, states = run_forward(info, packed, rows)
        heads = to_tokens(attended, rows).astype(f32)
        cot = features_whole(after(cotangent, packed))
        cot_keep, cot_send = pair_features(cot, rows)
        first_keep, first_send = pair_features(first, rows)
        gates = jnp.einsum("td,cdn->ctn", first, outgate_w, preferred_element_type=f32)
        gain_head = head_gain.astype(f32)
        inv_head = lax.rsqrt(jnp.mean(heads * heads, axis=-1, keepdims=True) + head_eps)
        unit = heads * inv_head
        sig_out = jax.nn.sigmoid(gates)
        silu_out = gates * sig_out
        mixed = (unit * gain_head * silu_out).astype(b16)
        residual = inputs + jnp.einsum("ctv,cdv->td", mixed, out_w, preferred_element_type=f32)
        inv_two = lax.rsqrt(jnp.mean(residual * residual, axis=1, keepdims=True) + norm_eps)
        normed_two = residual * inv_two
        second = (normed_two * gain_two).astype(b16)
        pre = jnp.einsum("td,cdn->ctn", second, late_w_hid, preferred_element_type=f32)
        gate_pre = pre[:, :, :hid]
        up_pre = pre[:, :, hid:]
        sig_gate = jax.nn.sigmoid(gate_pre)
        silu_gate = gate_pre * sig_gate
        hidden = (silu_gate * up_pre).astype(b16)

        hidden_pair = pair_tokens(hidden, rows)
        away_down = grad_part(cot_send, hidden_pair).astype(b16)
        came_down = swap(away_down, 2, rows)
        d_hidden = jnp.einsum("td,cdn->ctn", cot, down_w, preferred_element_type=f32)
        d_gate = d_hidden * up_pre * sig_gate * (1.0 + gate_pre * (1.0 - sig_gate))
        d_up = d_hidden * silu_gate
        d_pre = jnp.concatenate([d_gate.astype(b16), d_up.astype(b16)], axis=2)
        second_keep, second_send = pair_features(second, rows)
        pre_pair = pair_tokens(d_pre, rows)
        away_hid = grad_part(second_send, pre_pair).astype(b16)
        came_hid = swap(away_hid, 2, rows)
        out_rows = (
            residual + jnp.einsum("ctn,cdn->td", hidden, down_w, preferred_element_type=f32)
        ).astype(b16)
        d_second = jnp.einsum(
            "ctn,cdn->td", after(d_pre, away_down), late_w_hid, preferred_element_type=f32
        )
        part_two = jnp.sum(d_second * normed_two, axis=0)
        scaled_two = d_second * gain_two
        mean_two = jnp.mean(scaled_two * normed_two, axis=1, keepdims=True)
        d_resid = cot.astype(f32) + inv_two * (scaled_two - normed_two * mean_two)
        d_low = d_resid.astype(b16)
        d_low = after(d_low, away_hid)
        d_mixed = jnp.einsum("td,cdv->ctv", d_low, out_w, preferred_element_type=f32)
        gated = d_mixed * silu_out
        part_head = jnp.sum(gated * unit, axis=(0, 1))
        d_gates = d_mixed * unit * gain_head * sig_out * (1.0 + gates * (1.0 - sig_out))
        d_unit = gated * gain_head
        d_heads = inv_head * (d_unit - unit * jnp.mean(d_unit * unit, axis=-1, keepdims=True))
        d_gates = d_gates.astype(b16)
        total_down = (grad_part(cot_keep, hidden_pair) + came_down.astype(f32)).astype(b16)
        d_attended = to_heads(d_heads.astype(b16), rows)
        low_keep, low_send = pair_features(d_low, rows)
        mixed_pair = pair_tokens(mixed, rows)
        gates_pair = pair_tokens(d_gates, rows)
        away_out = jnp.concatenate(
            [grad_part(low_send, mixed_pair), grad_part(first_send, gates_pair)], axis=2
        ).astype(b16)
        came_out = swap(away_out, 2, rows)
        d_attended = after(d_attended, total_down, away_out)
        d_packed = run_backward(info, packed, d_attended, states, rows)
        grad_down = col_sum(total_down)
        d_packed = to_tokens(d_packed, rows)
        d_zeta = d_packed[:, :, narrow:].astype(f32)
        d_proj = d_packed[:, :, :narrow]
        d_rank = jnp.einsum("ctk,cks->ts", d_zeta, rank_out, precision=exact_mode)
        d_first = (
            jnp.einsum("ctn,cdn->td", d_proj, first_w, preferred_element_type=f32)
            + jnp.einsum("ctn,cdn->td", d_gates, outgate_w, preferred_element_type=f32)
            + lax.dot_general(
                d_rank, rank_in.astype(f32), NT, precision=exact_mode, preferred_element_type=f32
            )
        )
        part_one = jnp.sum(d_first * normed_one, axis=0)
        scaled_one = d_first * gain_one
        mean_one = jnp.mean(scaled_one * normed_one, axis=1, keepdims=True)
        grad_tokens = d_resid + inv_one * (scaled_one - normed_one * mean_one)
        part_rank_in = lax.dot_general(
            first.astype(f32), d_rank, TN, precision=exact_mode, preferred_element_type=f32
        )
        part_rank_out = jnp.einsum("ctk,ts->cks", d_zeta, rank_rows, precision=exact_mode)
        part_bias = jnp.sum(d_zeta, axis=1)
        row_side = jnp.concatenate(
            [part_rank_in, part_one[:, None], part_two[:, None]], axis=1
        ).reshape(1, rows, feat, RANK + 2)
        col_side = jnp.concatenate([part_rank_out, part_bias[:, :, None]], axis=2)
        col_side = jnp.pad(col_side, ((0, 0), (0, feat - HK), (0, 0)))[:, None]
        gain_side = part_head.reshape(1, 1, feat, 1)
        whole = (cols, rows, feat)
        side_grad = jnp.concatenate(
            [
                jnp.broadcast_to(row_side, whole + (RANK + 2,)),
                jnp.broadcast_to(col_side, whole + (RANK + 1,)),
                jnp.broadcast_to(gain_side, whole + (1,)),
                jnp.zeros(whole + (128 - 2 * RANK - 4,), f32),
            ],
            axis=3,
        ).astype(b16)

        def side_piece(bit):
            return lax.dynamic_index_in_dim(side_grad, me ^ bit, 1, False)

        side_other = swap(jnp.stack([side_piece(1), side_piece(3)]), 1, rows).astype(f32)
        side_keep = side_piece(0).astype(f32) + side_other[0]
        side_send = (side_piece(2).astype(f32) + side_other[1]).astype(b16)
        proj_pair = pair_tokens(d_proj, rows)
        away_first = grad_part(first_send, proj_pair).astype(b16)
        away_first = jnp.concatenate([away_first, side_send], axis=2)
        total_hid = (grad_part(second_keep, pre_pair) + came_hid.astype(f32)).astype(b16)
        grad_hid = col_sum(total_hid)
        held_out = jnp.concatenate(
            [grad_part(low_keep, mixed_pair), grad_part(first_keep, gates_pair)], axis=2
        )
        total_out = (held_out + came_out.astype(f32)).astype(b16)
        grad_out = col_sum(total_out)
        came_first = swap(after(away_first, total_hid), 2, rows)
        held_first = jnp.concatenate([grad_part(first_keep, proj_pair), side_keep], axis=2)
        grad_first = col_sum((held_first + came_first.astype(f32)).astype(b16))

        out_rows = exchange(out_rows.reshape(count, rows, feat).transpose(1, 0, 2))
        grad_tokens = exchange(
            grad_tokens.astype(b16).reshape(count, rows, feat).transpose(1, 0, 2)
        )
        grad_down = batch_sum(grad_down, dp)
        grad_hid = batch_sum(grad_hid, dp)
        grad_out = batch_sum(grad_out, dp)
        grad_first = batch_sum(grad_first, dp)
        side_sum = grad_first[:, narrow:]
        return (
            out_rows.reshape(rows * count, feat),
            grad_tokens.reshape(rows * count, feat).astype(f32),
            side_sum[:, RANK],
            grad_first[:, :HK],
            grad_first[:, HK : 2 * HK],
            grad_first[:, 2 * HK : narrow],
            grad_out[:, HV:],
            side_sum[:, :RANK],
            side_sum[:HK, RANK + 2 : 2 * RANK + 2].T,
            side_sum[:HK, 2 * RANK + 2],
            side_sum[:, 2 * RANK + 3],
            grad_out[:, :HV].T,
            side_sum[:, RANK + 1],
            grad_hid[:, :hid],
            grad_hid[:, hid:],
            grad_down.T,
        )

    return per_device


def solution(mesh):
    grid = P("row", "col")
    flipped = P("col", "row")
    tokens = P(("dp", "col"), "row")
    in_specs = (
        tokens,
        tokens,
        P(("dp", "row"), None),
        P("row"),
        grid,
        grid,
        grid,
        grid,
        P("row", None),
        P(None, "col"),
        P("col"),
        P(),
        flipped,
        P("row"),
        grid,
        grid,
        flipped,
    )
    out_specs = (
        tokens,
        tokens,
        P("row"),
        grid,
        grid,
        grid,
        grid,
        P("row", None),
        P(None, "col"),
        P("col"),
        P(),
        flipped,
        P("row"),
        grid,
        grid,
        flipped,
    )
    body = make_body(mesh.shape["dp"], mesh.shape["row"], mesh.shape["col"])

    return jax.shard_map(body, mesh=mesh, in_specs=in_specs, out_specs=out_specs, check_vma=False)
```

```python
import jax
import jax.numpy as jnp
from jax import lax
from jax.experimental import pallas as pl
from jax.experimental.pallas import tpu as pltpu
from jax.sharding import PartitionSpec as P


D = 1024
SPAN = 64
HK = 128
HV = 256
RANK = 16

exact_mode = lax.Precision.HIGHEST
norm_eps = 1e-05
head_eps = 1.0
f32 = jnp.float32
b16 = jnp.bfloat16
GRID = ("col", "row")
NT = (((1,), (1,)), ((), ()))
TN = (((0,), (0,)), ((), ()))


def dot(left, right, dims=(((1,), (0,)), ((), ()))):
    return lax.dot_general(left, right, dims, preferred_element_type=f32)


def exchange(blocks):
    return lax.all_to_all(blocks, "row", 0, 0)


def span_parts(starts_ref, base, x):
    docs = starts_ref.shape[0] - 2
    rows = lax.broadcasted_iota(jnp.int32, (SPAN, HK), 0) + base
    first = jnp.zeros((SPAN, HK), jnp.int32)
    last_first = jnp.int32(0)
    for d in range(docs):
        s = starts_ref[d]
        first = jnp.where(rows >= s, jnp.maximum(first, s), first)
        last_first = jnp.where(base + SPAN - 1 >= s, jnp.maximum(last_first, s), last_first)
    i = lax.broadcasted_iota(jnp.int32, (SPAN, SPAN), 0)
    j = lax.broadcasted_iota(jnp.int32, (SPAN, SPAN), 1)
    allowed = (j <= i) & (j + base >= first[:, :SPAN])
    reads = (first < base).astype(f32)
    tail = (rows >= last_first).astype(f32)
    keep = (last_first < base).astype(f32)
    q = x[:, :HK].astype(f32) * HK ** (-0.5)
    k = x[:, HK : 2 * HK].astype(f32)
    v = x[:, 2 * HK : 2 * HK + HV]
    lam = x[:, 2 * HK + HV :]
    tri = (j <= i).astype(b16)
    cum = dot(tri, lam)
    final = cum[SPAN - 1 :, :]
    e_pos = jnp.exp(cum)
    e_neg = jnp.exp(-cum)
    e_end = jnp.exp(final - cum)
    qs = (q * e_pos).astype(b16)
    ks = (k * e_neg).astype(b16)
    ke = (k * e_end * tail).astype(b16)
    qr = (qs.astype(f32) * reads).astype(b16)
    fade = jnp.exp(final) * keep
    scores = jnp.where(allowed, dot(qs, ks, NT), 0.0).astype(b16)
    return v, lam, e_pos, e_neg, e_end, qs, ks, ke, qr, fade, scores, allowed, reads, tail, i, j


def span_base(info_ref, block, n):
    docs = info_ref.shape[0] - 2
    return info_ref[docs] * (2 * BLOCK) + block * BLOCK + n * SPAN


def mix_state(info_ref, x_ref, end_ref, carry_ref):
    block = pl.program_id(1)

    @pl.when(block == 0)
    def _():
        carry_ref[...] = jnp.zeros_like(carry_ref)

    state = carry_ref[...]
    for n in range(BLOCK // SPAN):
        part = span_parts(info_ref, span_base(info_ref, block, n), x_ref[pl.ds(n * SPAN, SPAN), :])
        state = state * part[9] + dot(part[0], part[7], TN)
    carry_ref[...] = state
    end_ref[...] = state


def mix_forward(info_ref, x_ref, start_ref, o_ref, states_ref, carry_ref):
    block = pl.program_id(1)

    @pl.when(block == 0)
    def _():
        carry_ref[...] = start_ref[...]

    state = carry_ref[...]
    for n in range(BLOCK // SPAN):
        at = pl.ds(n * SPAN, SPAN)
        part = span_parts(info_ref, span_base(info_ref, block, n), x_ref[at, :])
        v, ke, qr, fade, scores = part[0], part[7], part[8], part[9], part[10]
        low = state.astype(b16)
        states_ref[n] = low
        o_ref[at, :] = (dot(scores, v) + dot(qr, low, NT)).astype(b16)
        state = state * fade + dot(v, ke, TN)
    carry_ref[...] = state


def mix_grad_state(info_ref, x_ref, do_ref, end_ref, carry_ref):
    step = pl.program_id(1)

    @pl.when(step == 0)
    def _():
        carry_ref[...] = jnp.zeros_like(carry_ref)

    grad = carry_ref[...]
    for n in reversed(range(BLOCK // SPAN)):
        at = pl.ds(n * SPAN, SPAN)
        part = span_parts(info_ref, span_base(info_ref, 1 - step, n), x_ref[at, :])
        grad = grad * part[9] + dot(do_ref[at, :], part[8], TN)
    carry_ref[...] = grad
    end_ref[...] = grad


def mix_backward(info_ref, x_ref, do_ref, states_ref, start_ref, out_ref, carry_ref):
    step = pl.program_id(1)

    @pl.when(step == 0)
    def _():
        carry_ref[...] = start_ref[...]

    grad = carry_ref[...]
    for n in reversed(range(BLOCK // SPAN)):
        at = pl.ds(n * SPAN, SPAN)
        (v, lam, e_pos, e_neg, e_end, qs, ks, ke, qr, fade, scores, allowed, reads, tail, i, j) = (
            span_parts(info_ref, span_base(info_ref, 1 - step, n), x_ref[at, :])
        )
        do = do_ref[at, :]
        low = grad.astype(b16)
        before = states_ref[n]
        d_scores = jnp.where(allowed, dot(do, v, NT), 0.0).astype(b16)
        dv = dot(scores, do, TN) + dot(ke, low, NT)
        dqs = dot(d_scores, ks) + dot(do, before) * reads
        dks = dot(d_scores, qs, TN)
        dke = dot(v, low) * tail
        d_fade = jnp.sum(before.astype(f32) * grad, axis=0, keepdims=True)
        grad = grad * fade + dot(do, qr, TN)
        end_part = dke * ke.astype(f32)
        d_cum = dqs * qs.astype(f32) - dks * ks.astype(f32) - end_part
        d_final = jnp.sum(end_part, axis=0, keepdims=True) + d_fade * fade
        upper = (j >= i).astype(b16)
        high = d_cum.astype(b16)
        rest = (d_cum - high.astype(f32)).astype(b16)
        d_lam = dot(upper, high) + dot(upper, rest) + d_final
        d_zeta = d_lam * ((1.0 - jnp.exp(lam.astype(f32) * 16.0)) / 16.0)
        out_ref[at, :HK] = (dqs * e_pos * HK ** (-0.5)).astype(b16)
        out_ref[at, HK : 2 * HK] = (dks * e_neg + dke * e_end).astype(b16)
        out_ref[at, 2 * HK : 2 * HK + HV] = dv.astype(b16)
        out_ref[at, 2 * HK + HV :] = d_zeta.astype(b16)
    carry_ref[...] = grad


BLOCK = 512


def run_mix(kernel, reverse, work, info, operands, results):
    heads = operands[0].shape[1]

    def order(step):
        return 1 - step if reverse else step

    def spec(array):
        if len(array.shape) == 4:
            return pl.BlockSpec(
                (None, None) + array.shape[2:],
                lambda h, s, info_ref: (order(s) ^ info_ref[info_ref.shape[0] - 1], h, 0, 0),
            )
        if len(array.shape) == 5:
            return pl.BlockSpec(
                (None, None) + array.shape[2:], lambda h, s, info_ref: (order(s), h, 0, 0, 0)
            )
        return pl.BlockSpec((None,) + array.shape[1:], lambda h, s, info_ref: (h, 0, 0))

    return pl.pallas_call(
        kernel,
        out_shape=results,
        grid_spec=pltpu.PrefetchScalarGridSpec(
            num_scalar_prefetch=1,
            grid=(heads, 2),
            in_specs=[spec(array) for array in operands],
            out_specs=tuple(spec(array) for array in results),
            scratch_shapes=[pltpu.VMEM((HV, HK), f32)],
        ),
        cost_estimate=pl.CostEstimate(
            flops=work * 200000000, bytes_accessed=work * 4000000, transcendentals=work * 800000
        ),
    )(info, *operands)


def run_forward(info, packed):
    pairs, heads, count = packed.shape[:3]
    state = jax.ShapeDtypeStruct((heads, HV, HK), f32)
    (end,) = run_mix(mix_state, False, 1, info, (packed,), (state,))
    begin = lax.ppermute(end, "row", [(0, 2), (1, 3)])
    out = jax.ShapeDtypeStruct((pairs, heads, count, HV), b16)
    kept = jax.ShapeDtypeStruct((pairs, heads, count // SPAN, HV, HK), b16)
    return run_mix(mix_forward, False, 2, info, (packed, begin), (out, kept))


def run_backward(info, packed, d_out, states, firsts):
    _, heads, _ = packed.shape[:3]
    state = jax.ShapeDtypeStruct((heads, HV, HK), f32)
    (end,) = run_mix(mix_grad_state, True, 1, info, (packed, d_out), (state,))
    begin = lax.ppermute(end, "row", [(2, 0), (3, 1)])
    begin = after(begin, *firsts)
    out = jax.ShapeDtypeStruct(packed.shape, b16)
    return run_mix(mix_backward, True, 4, info, (packed, d_out, states, begin), (out,))[0]


def gather_blocks(block, rows, cols):
    whole = lax.all_gather(block, GRID, axis=0, tiled=True)
    return whole.reshape(cols, rows, block.shape[0], block.shape[1])


def batch_sum(part, pair):
    if pair == 2:
        other = lax.ppermute(part, "dp", [(0, 1), (1, 0)])
        return part.astype(f32) + other.astype(f32)
    return lax.psum(part, "dp").astype(f32)


def swap(part, bit, rows):
    return lax.ppermute(part, "row", [(i, i ^ bit) for i in range(rows)])


def pair_features(whole, rows):
    feat = whole.shape[1] // rows
    me = lax.axis_index("row")

    def piece(bit):
        return lax.dynamic_slice_in_dim(whole, (me ^ bit) * feat, feat, 1)

    other = swap(jnp.stack([piece(1), piece(3)]), 1, rows)
    keep = jnp.concatenate([piece(0), other[0]], axis=0)
    send = jnp.concatenate([piece(2), other[1]], axis=0)
    return keep, send


def pair_tokens(blocks, rows):
    return jnp.concatenate([blocks, swap(blocks, 1, rows)], axis=1)


def to_heads(blocks, rows):
    parts = blocks.reshape((2, -1) + blocks.shape[1:])
    core = lax.axis_index("row") % 2
    mine = lax.dynamic_index_in_dim(parts, core, 0, False)
    away = lax.dynamic_index_in_dim(parts, 1 - core, 0, False)
    return jnp.stack([mine, swap(away, 1, rows)])


def to_tokens(parts, rows):
    other = swap(parts[1], 1, rows)
    core = lax.axis_index("row") % 2
    both = jnp.where(
        core == 0, jnp.stack([parts[0], other]), jnp.stack([other, parts[0]])
    )
    return both.reshape((-1,) + both.shape[2:])


def grad_part(features, blocks):
    return jnp.einsum("td,ctn->cdn", features, blocks, preferred_element_type=f32)


def joined(held, came):
    total = (held + came.astype(f32)).astype(b16)
    return total.reshape(-1, total.shape[-1])


def col_sum(total):
    return lax.psum_scatter(total, "col", scatter_dimension=0, tiled=True)


def after(value, *firsts):
    return lax.optimization_barrier((value,) + firsts)[0]


def make_body(dp, rows, cols):
    def per_device(
        tokens_in,
        cotangent,
        doc_lengths,
        mixer_gain,
        w_query,
        w_key,
        w_value,
        w_outgate,
        w_rank_in,
        w_rank_out,
        decay_bias,
        head_gain,
        w_output,
        ffn_gain,
        w_gate,
        w_up,
        w_down,
    ):
        feat = tokens_in.shape[1]
        count = tokens_in.shape[0] // rows
        narrow = 2 * HK + HV
        cross = [(a * cols + b, b * cols + a) for a in range(rows) for b in range(cols)]
        lengths = lax.ppermute(doc_lengths, ("row", "col"), cross)[0]
        starts = jnp.cumsum(lengths, dtype=jnp.int32) - lengths
        me = lax.axis_index("row")
        info = jnp.concatenate([starts, jnp.stack([me // 2, me % 2]).astype(jnp.int32)])
        key_side = jnp.concatenate([w_rank_out.T, decay_bias[:, None]], axis=1)
        side = jnp.concatenate(
            [
                w_rank_in,
                mixer_gain[:, None],
                ffn_gain[:, None],
                jnp.pad(key_side, ((0, feat - HK), (0, 0))),
                jnp.zeros((feat, 128 - 2 * RANK - 3), b16),
            ],
            axis=1,
        )
        first_w = gather_blocks(
            jnp.concatenate([w_query, w_key, w_value, side], axis=1), rows, cols
        )
        late_w = gather_blocks(
            jnp.concatenate(
                [
                    w_gate,
                    w_up,
                    w_output.T,
                    w_outgate,
                    w_down.T,
                    jnp.zeros((feat, -(3 * w_gate.shape[1]) % 128), b16),
                ],
                axis=1,
            ),
            rows,
            cols,
        )
        extra = first_w[0, :, :, narrow:].reshape(D, 128)
        rank_in = extra[:, :RANK]
        gain_one = extra[:, RANK].astype(f32)
        gain_two = extra[:, RANK + 1].astype(f32)
        keys_extra = first_w[:, 0, :HK, narrow:]
        rank_out = keys_extra[:, :, RANK + 2 : 2 * RANK + 2].astype(f32)
        bias = keys_extra[:, :, 2 * RANK + 2].astype(f32)
        first_w = first_w.reshape(cols, D, narrow + 128)[:, :, :narrow]

        def features_whole(block):
            split = exchange(block.reshape(rows, count, feat))
            return split.transpose(1, 0, 2).reshape(count, D)

        inputs = features_whole(tokens_in).astype(f32)
        inv_one = lax.rsqrt(jnp.mean(inputs * inputs, axis=1, keepdims=True) + norm_eps)
        normed_one = inputs * inv_one
        first = (normed_one * gain_one).astype(b16)
        proj = jnp.einsum("td,cdn->ctn", first, first_w, preferred_element_type=f32)
        rank_rows = dot(first, rank_in)
        zeta = (
            jnp.einsum("ts,cks->ctk", rank_rows, rank_out, precision=exact_mode)
            + bias[:, None, :]
        )
        lam = jax.nn.log_sigmoid(zeta) / 16.0
        packed = jnp.concatenate([proj, lam], axis=2).astype(b16)
        packed = to_heads(packed, rows)
        attended, states = run_forward(info, packed)
        heads = to_tokens(attended, rows).astype(f32)
        cot = features_whole(after(cotangent, packed))
        cot_keep, cot_send = pair_features(cot, rows)
        first_keep, first_send = pair_features(first, rows)
        late_w = after(late_w, cot_keep, cot_send, first_keep, first_send)
        late_w = late_w.reshape(cols, D, -1)
        hid = w_gate.shape[1]
        late_w_hid = late_w[:, :, : 2 * hid]
        out_w = late_w[:, :, 2 * hid : 2 * hid + HV]
        outgate_w = late_w[:, :, 2 * hid + HV : 2 * hid + 2 * HV]
        down_w = late_w[:, :, 2 * hid + 2 * HV : 3 * hid + 2 * HV]
        gates = jnp.einsum("td,cdn->ctn", first, outgate_w, preferred_element_type=f32)
        gain_head = head_gain.astype(f32)
        inv_head = lax.rsqrt(jnp.mean(heads * heads, axis=-1, keepdims=True) + head_eps)
        unit = heads * inv_head
        sig_out = jax.nn.sigmoid(gates)
        silu_out = gates * sig_out
        mixed = (unit * gain_head * silu_out).astype(b16)
        residual = inputs + jnp.einsum("ctv,cdv->td", mixed, out_w, preferred_element_type=f32)
        inv_two = lax.rsqrt(jnp.mean(residual * residual, axis=1, keepdims=True) + norm_eps)
        normed_two = residual * inv_two
        second = (normed_two * gain_two).astype(b16)
        pre = jnp.einsum("td,cdn->ctn", second, late_w_hid, preferred_element_type=f32)
        gate_pre = pre[:, :, :hid]
        up_pre = pre[:, :, hid:]
        sig_gate = jax.nn.sigmoid(gate_pre)
        silu_gate = gate_pre * sig_gate
        hidden = (silu_gate * up_pre).astype(b16)

        hidden_pair = pair_tokens(hidden, rows)
        away_down = grad_part(cot_send, hidden_pair).astype(b16)
        came_down = swap(away_down, 2, rows)
        d_hidden = jnp.einsum("td,cdn->ctn", cot, down_w, preferred_element_type=f32)
        d_gate = d_hidden * up_pre * sig_gate * (1.0 + gate_pre * (1.0 - sig_gate))
        d_up = d_hidden * silu_gate
        d_gate = d_gate.astype(b16)
        d_up = d_up.astype(b16)
        d_pre = jnp.concatenate([d_gate, d_up], axis=2)
        second_keep, second_send = pair_features(second, rows)
        gate_pair = pair_tokens(d_gate, rows)
        up_pair = pair_tokens(d_up, rows)
        away_gate = grad_part(second_send, gate_pair).astype(b16)
        came_gate = swap(away_gate, 2, rows)
        away_up = grad_part(second_send, up_pair).astype(b16)
        came_up = swap(away_up, 2, rows)
        out_rows = (
            residual + jnp.einsum("ctn,cdn->td", hidden, down_w, preferred_element_type=f32)
        ).astype(b16)
        d_pre = after(d_pre, away_down)
        d_second = jnp.einsum("ctn,cdn->td", d_pre, late_w_hid, preferred_element_type=f32)
        part_two = jnp.sum(d_second * normed_two, axis=0)
        scaled_two = d_second * gain_two
        mean_two = jnp.mean(scaled_two * normed_two, axis=1, keepdims=True)
        d_resid = cot.astype(f32) + inv_two * (scaled_two - normed_two * mean_two)
        d_low = d_resid.astype(b16)
        d_low = after(d_low, away_gate)
        d_mixed = jnp.einsum("td,cdv->ctv", d_low, out_w, preferred_element_type=f32)
        gated = d_mixed * silu_out
        part_head = jnp.sum(gated * unit, axis=(0, 1))
        d_gates = d_mixed * unit * gain_head * sig_out * (1.0 + gates * (1.0 - sig_out))
        d_unit = gated * gain_head
        d_heads = inv_head * (d_unit - unit * jnp.mean(d_unit * unit, axis=-1, keepdims=True))
        d_gates = d_gates.astype(b16)
        total_down = joined(grad_part(cot_keep, hidden_pair), came_down)
        d_attended = to_heads(d_heads.astype(b16), rows)
        low_keep, low_send = pair_features(d_low, rows)
        mixed_pair = pair_tokens(mixed, rows)
        gates_pair = pair_tokens(d_gates, rows)
        away_out = jnp.concatenate(
            [grad_part(low_send, mixed_pair), grad_part(first_send, gates_pair)], axis=2
        ).astype(b16)
        came_out = swap(away_out, 2, rows)
        d_attended = after(d_attended, total_down, away_up, away_out)
        grad_down = col_sum(total_down)
        total_gate = joined(grad_part(second_keep, gate_pair), came_gate)
        d_packed = run_backward(info, packed, d_attended, states, (total_gate,))
        grad_gate = col_sum(total_gate)
        d_packed = to_tokens(d_packed, rows)
        d_zeta = d_packed[:, :, narrow:].astype(f32)
        d_proj = d_packed[:, :, :narrow]
        d_rank = jnp.einsum("ctk,cks->ts", d_zeta, rank_out, precision=exact_mode)
        d_first = (
            jnp.einsum("ctn,cdn->td", d_proj, first_w, preferred_element_type=f32)
            + jnp.einsum("ctn,cdn->td", d_gates, outgate_w, preferred_element_type=f32)
            + lax.dot_general(
                d_rank, rank_in.astype(f32), NT, precision=exact_mode, preferred_element_type=f32
            )
        )
        part_one = jnp.sum(d_first * normed_one, axis=0)
        scaled_one = d_first * gain_one
        mean_one = jnp.mean(scaled_one * normed_one, axis=1, keepdims=True)
        grad_tokens = d_resid + inv_one * (scaled_one - normed_one * mean_one)
        part_rank_in = lax.dot_general(
            first.astype(f32), d_rank, TN, precision=exact_mode, preferred_element_type=f32
        )
        part_rank_out = jnp.einsum("ctk,ts->cks", d_zeta, rank_rows, precision=exact_mode)
        part_bias = jnp.sum(d_zeta, axis=1)
        row_side = jnp.concatenate(
            [part_rank_in, part_one[:, None], part_two[:, None]], axis=1
        ).reshape(1, rows, feat, RANK + 2)
        col_side = jnp.concatenate([part_rank_out, part_bias[:, :, None]], axis=2)
        col_side = jnp.pad(col_side, ((0, 0), (0, feat - HK), (0, 0)))[:, None]
        gain_side = part_head.reshape(1, 1, feat, 1)
        whole = (cols, rows, feat)
        side_grad = jnp.concatenate(
            [
                jnp.broadcast_to(row_side, whole + (RANK + 2,)),
                jnp.broadcast_to(col_side, whole + (RANK + 1,)),
                jnp.broadcast_to(gain_side, whole + (1,)),
                jnp.zeros(whole + (128 - 2 * RANK - 4,), f32),
            ],
            axis=3,
        ).astype(b16)

        def side_piece(bit):
            return lax.dynamic_index_in_dim(side_grad, me ^ bit, 1, False)

        side_other = swap(jnp.stack([side_piece(1), side_piece(3)]), 1, rows).astype(f32)
        side_keep = side_piece(0).astype(f32) + side_other[0]
        side_send = (side_piece(2).astype(f32) + side_other[1]).astype(b16)
        proj_pair = pair_tokens(d_proj, rows)
        away_first = grad_part(first_send, proj_pair).astype(b16)
        away_first = jnp.concatenate([away_first, side_send], axis=2)
        total_up = joined(grad_part(second_keep, up_pair), came_up)
        grad_up = col_sum(total_up)
        held_out = jnp.concatenate(
            [grad_part(low_keep, mixed_pair), grad_part(first_keep, gates_pair)], axis=2
        )
        total_out = joined(held_out, came_out)
        grad_out = col_sum(total_out)
        came_first = swap(after(away_first, total_up, total_out), 2, rows)
        held_first = jnp.concatenate([grad_part(first_keep, proj_pair), side_keep], axis=2)
        grad_first = col_sum(joined(held_first, came_first))

        out_rows = exchange(out_rows.reshape(count, rows, feat).transpose(1, 0, 2))
        grad_tokens = exchange(
            grad_tokens.astype(b16).reshape(count, rows, feat).transpose(1, 0, 2)
        )
        grad_down = batch_sum(grad_down, dp)
        grad_gate = batch_sum(grad_gate, dp)
        grad_up = batch_sum(grad_up, dp)
        grad_out = batch_sum(grad_out, dp)
        grad_first = batch_sum(grad_first, dp)
        side_sum = grad_first[:, narrow:]
        return (
            out_rows.reshape(rows * count, feat),
            grad_tokens.reshape(rows * count, feat).astype(f32),
            side_sum[:, RANK],
            grad_first[:, :HK],
            grad_first[:, HK : 2 * HK],
            grad_first[:, 2 * HK : narrow],
            grad_out[:, HV:],
            side_sum[:, :RANK],
            side_sum[:HK, RANK + 2 : 2 * RANK + 2].T,
            side_sum[:HK, 2 * RANK + 2],
            side_sum[:, 2 * RANK + 3],
            grad_out[:, :HV].T,
            side_sum[:, RANK + 1],
            grad_gate,
            grad_up,
            grad_down.T,
        )

    return per_device


def solution(mesh):
    grid = P("row", "col")
    flipped = P("col", "row")
    tokens = P(("dp", "col"), "row")
    in_specs = (
        tokens,
        tokens,
        P(("dp", "row"), None),
        P("row"),
        grid,
        grid,
        grid,
        grid,
        P("row", None),
        P(None, "col"),
        P("col"),
        P(),
        flipped,
        P("row"),
        grid,
        grid,
        flipped,
    )
    out_specs = (
        tokens,
        tokens,
        P("row"),
        grid,
        grid,
        grid,
        grid,
        P("row", None),
        P(None, "col"),
        P("col"),
        P(),
        flipped,
        P("row"),
        grid,
        grid,
        flipped,
    )
    body = make_body(mesh.shape["dp"], mesh.shape["row"], mesh.shape["col"])

    return jax.shard_map(body, mesh=mesh, in_specs=in_specs, out_specs=out_specs, check_vma=False)
```
